256 devices in a mesh: tm: 4 (over x), rows: 32 (over z, y), clip: 2 (over core).
Axes of the slice: x: 4, y: 4, z: 8, core: 2. Of those that a mesh axis runs over, the one named last changes fastest.
Arguments:
- features: bfloat16 [8, 16, 64, 9984], P('clip', 'tm', 'rows'), may hold values from -6 to 6
- lengths: int32 [8], replicated, may hold values from 1 to 16, as said below
- stored_slot: int32 [8], replicated, may hold values from 0 to 7, each once
- owner_slot: int32 [8], replicated, may hold values from 0 to 7, each once
- gain_first: float32 [96], replicated, may hold values from 0.1 to 1.9
- conv_first: bfloat16 [3, 3, 3, 96, 96], replicated, may hold values from -0.125 to 0.125
- bias_first: float32 [96], replicated, may hold values from -3 to 3
- gain_second: float32 [96], replicated, may hold values from 0.1 to 1.9
- conv_second: bfloat16 [3, 3, 3, 96, 96], replicated, may hold values from -0.125 to 0.125
- bias_second: float32 [96], replicated, may hold values from -3 to 3
- reduce_conv_weight: bfloat16 [3, 3, 96, 96], replicated, may hold values from -0.21875 to 0.21875
- reduce_conv_bias: float32 [96], replicated, may hold values from -3 to 3
Outputs:
- encoded: bfloat16 [8, 16, 32, 4992], P('clip', 'tm', 'rows')
The draws below stay inside these ranges and needn't reach their ends.
Inputs may be any that keep to these rules, and one draw needn't show every extreme that they name: `lengths`: some clip has all 16 frames. `stored_slot`: each clip has its own storage slot. `owner_slot`: each clip has its own output slot.
All inputs are finite; a program needn't handle non-finite values.
Results may differ from the reference program's by a relative error of at most 0.0051.
Values may be sent and summed in bfloat16 or wider, within the bound.
A program may use at most 64 MiB of HBM per device.

```python
import jax
import jax.numpy as jnp
from jax import lax

CHANNELS = 96
WIDTH = 104
FRAMES = 16
HEIGHT = 64
CLIPS = 8


def draw_lengths(key, part):
    first_key, second_key = jax.random.split(key)
    base_len = jax.random.randint(first_key, (CLIPS,), 1, FRAMES + 1)
    full_clip = jax.random.randint(second_key, (), 0, CLIPS)
    return jnp.where(jnp.arange(CLIPS) == full_clip, FRAMES, base_len).astype(jnp.int32)


def levels(key, shape, shards, low, top_value):
    def one(dim, shards_of):
        heights = jax.random.uniform(jax.random.fold_in(jax.random.fold_in(key, 6), dim), (shards_of,), jnp.float32, low / len(shards), top_value / len(shards))
        return jnp.repeat(jnp.exp(heights), shape[dim] // shards_of).reshape((-1,) + (1,) * (len(shape) - dim - 1))

    level = one(*shards[0])
    for cut in shards[1:]:
        level = level * one(*cut)
    return level


def normal_values(key, shape, scale, bound, cuts=(), kind=jnp.bfloat16):
    values = jax.random.normal(key, shape, jnp.float32) * scale
    if len(cuts) > 0:
        values = levels(key, shape, cuts, -0.22, 0.18) * values
    return jnp.clip(values, min=-bound, max=bound).astype(kind)


def setup_inputs(seed: int = 0) -> dict:
    splits = jax.random.split(jax.random.key(seed), 13)
    features = normal_values(splits[0], (CLIPS, FRAMES, HEIGHT, WIDTH * CHANNELS), 1.0, 6.0, ((0, 2), (1, 4), (2, 32)))
    lengths = draw_lengths(jax.random.fold_in(splits[12], 71), 0)
    stored_slot = jax.random.permutation(splits[2], CLIPS).astype(jnp.int32)
    owner_slot = jax.random.permutation(splits[3], CLIPS).astype(jnp.int32)
    gain_first = jnp.clip(1.0 + 0.18 * jax.random.normal(splits[4], (CHANNELS,), jnp.float32), 0.1, 1.9)
    conv_first = normal_values(splits[5], (3, 3, 3, CHANNELS, CHANNELS), (27 * CHANNELS) ** -0.5, 0.125)
    bias_first = normal_values(splits[6], (CHANNELS,), 0.5, 3.0, (), jnp.float32)
    gain_second = jnp.clip(1.0 + 0.18 * jax.random.normal(splits[7], (CHANNELS,), jnp.float32), 0.1, 1.9)
    conv_second = normal_values(splits[8], (3, 3, 3, CHANNELS, CHANNELS), (27 * CHANNELS) ** -0.5, 0.125)
    bias_second = normal_values(splits[9], (CHANNELS,), 0.5, 3.0, (), jnp.float32)
    reduce_conv_weight = normal_values(splits[10], (3, 3, CHANNELS, CHANNELS), (9 * CHANNELS) ** -0.5, 0.21875)
    reduce_conv_bias = normal_values(splits[11], (CHANNELS,), 0.5, 3.0, (), jnp.float32)
    return {"features": features, "lengths": lengths, "stored_slot": stored_slot, "owner_slot": owner_slot, "gain_first": gain_first, "conv_first": conv_first, "bias_first": bias_first, "gain_second": gain_second, "conv_second": conv_second, "bias_second": bias_second, "reduce_conv_weight": reduce_conv_weight, "reduce_conv_bias": reduce_conv_bias}


NORM_EPS = 1e-06

def norm_silu(values, gain_vec):
    scaled = values * lax.rsqrt(lax.optimization_barrier(jnp.mean(values * values, axis=-1, keepdims=True)) + NORM_EPS) * gain_vec
    return jax.nn.silu(scaled)

def conv_valid(grown_block, kernel_weight, bias_vector):
    frames = grown_block.shape[0] - 2
    band_rows = grown_block.shape[1] - 2
    columns = grown_block.shape[2]
    channels = grown_block.shape[3]
    outputs = kernel_weight.shape[4]
    padded = jnp.pad(grown_block, ((0, 0), (0, 0), (1, 1), (0, 0)))
    running_sum = jnp.zeros((frames * band_rows * columns, outputs), jnp.float32)
    for step_t in range(3):
        for step_h in range(3):
            window = padded[step_t:step_t + frames, step_h:step_h + band_rows]
            tap_stack = jnp.concatenate([window[:, :, step_w:step_w + columns] for step_w in range(3)], axis=-1)
            running_sum = running_sum + jnp.dot(tap_stack.reshape(-1, 3 * channels), kernel_weight[step_t, step_h].reshape(3 * channels, outputs), preferred_element_type=jnp.float32)
    return (running_sum + bias_vector).reshape(frames, band_rows, columns, outputs)

def spatial_reduce(padded_frames, kernel_weight, bias_vector):
    frames = padded_frames.shape[0]
    half_rows = (padded_frames.shape[1] - 1) // 2
    columns = padded_frames.shape[2]
    channels = padded_frames.shape[3]
    outputs = kernel_weight.shape[3]
    padded = jnp.pad(padded_frames, ((0, 0), (0, 0), (0, 1), (0, 0)))
    running_sum = jnp.zeros((frames * half_rows * (columns // 2), outputs), jnp.float32)
    for step_h in range(3):
        row_band = padded[:, step_h:step_h + 2 * half_rows - 1:2]
        tap_stack = jnp.concatenate([row_band[:, :, step_w:step_w + columns - 1:2] for step_w in range(3)], axis=-1)
        running_sum = running_sum + jnp.dot(tap_stack.reshape(-1, 3 * channels), kernel_weight[step_h].reshape(3 * channels, outputs), preferred_element_type=jnp.float32)
    return (running_sum + bias_vector).reshape(frames, half_rows, columns // 2, outputs)

def encode_clip(feature_map, length, gain_first, conv_first, bias_first, gain_second, conv_second, bias_second, reduce_conv_weight, reduce_conv_bias):
    first_act = norm_silu(feature_map.astype(jnp.float32), gain_first).astype(jnp.bfloat16)
    first_conv = conv_valid(jnp.pad(first_act, ((2, 0), (1, 1), (0, 0), (0, 0))), conv_first, bias_first)
    second_act = norm_silu(first_conv, gain_second).astype(jnp.bfloat16)
    branch = conv_valid(jnp.pad(second_act, ((2, 0), (1, 1), (0, 0), (0, 0))), conv_second, bias_second)
    residual_block_output = (feature_map.astype(jnp.float32) + branch).astype(jnp.bfloat16)
    spatial_reduced = spatial_reduce(jnp.pad(residual_block_output, ((0, 0), (0, 1), (0, 0), (0, 0))), reduce_conv_weight, reduce_conv_bias)
    alive_frame = jnp.arange(feature_map.shape[0], dtype=jnp.int32) < length
    return jnp.where(alive_frame[:, None, None, None], spatial_reduced, 0.0).astype(jnp.bfloat16)

def reference(features, lengths, stored_slot, owner_slot, gain_first, conv_first, bias_first, gain_second, conv_second, bias_second, reduce_conv_weight, reduce_conv_bias):

    def encode_one(clip_number):
        clip_data = features[stored_slot[clip_number]].reshape(FRAMES, HEIGHT, WIDTH, CHANNELS)
        result = encode_clip(clip_data, lengths[clip_number], gain_first, conv_first, bias_first, gain_second, conv_second, bias_second, reduce_conv_weight, reduce_conv_bias)
        return result.reshape(FRAMES, HEIGHT // 2, WIDTH // 2 * CHANNELS)
    results = lax.map(encode_one, jnp.arange(CLIPS, dtype=jnp.int32))
    inverse = jnp.zeros((CLIPS,), jnp.int32).at[owner_slot].set(jnp.arange(CLIPS, dtype=jnp.int32))
    return results[inverse]
```

```python
import jax
import jax.numpy as jnp
from jax import lax
from jax.experimental import pallas as pl
from jax.experimental.pallas import tpu as pltpu
from jax.sharding import PartitionSpec as P

NORM_EPS = 1e-06
MESH = pl.DeviceIdType.MESH
F32 = jnp.float32
BF16 = jnp.bfloat16

CH = 96
XB = 4
YB = 4
ZB = 8
OWN = 26
GROUPS = 9
WIN = GROUPS * 4
PADL = 384
PADR = 768
LANES = 128
PAIRS1 = 15
PAIRS2 = 14
BC = 2 * PAIRS1
OC = 2 * PAIRS2
JC = 13


def lane_iota(shape):
    return lax.broadcasted_iota(jnp.int32, shape, len(shape) - 1)


def shifted(flat, step, frame):
    return jnp.where(frame < step, 0.0, pltpu.roll(flat, step, 0))


def silu(u):
    return 0.5 * u * (1.0 + jnp.tanh(0.5 * u))


def norm_act(v, gain):
    mean = jnp.sum(v * v, axis=-1, keepdims=True) * (1.0 / CH)
    return silu(v * lax.rsqrt(mean + NORM_EPS) * gain)


def build_toeplitz(w_ref, wt):
    wt[...] = jnp.zeros_like(wt)

    def tap(i, _):
        for n in range(2):
            for k in range(3):
                wt[i, pl.ds(128 * (n + k), CH), pl.ds(128 * n, CH)] = w_ref[3 * i + k]
        return 0

    lax.fori_loop(0, 9, tap, 0)


def conv_lhs(src, base, p0, pairs, rows):
    parts = []
    for t in range(3):
        for j in range(3):
            for k in range(4):
                pieces = [
                    src[t, base + 2 * (p0 + p) + k, j : j + rows].reshape(rows * 16, LANES)
                    for p in range(pairs)
                ]
                parts.append(jnp.concatenate(pieces, axis=0))
    return jnp.concatenate(parts, axis=1)


def kernel(
    feat, w1, w2, wr, g1, b1, g2, b2, br, lengths, stored, owner, out,
    arr, xs, a, b, wt1, wt2, rw, ob, sb, gb, ha, hb, ho,
    s_a, r_a, s_z, r_z, s_g, r_g, s_c, r_c, l_sem,
):
    x = lax.axis_index("tm")
    zy = lax.axis_index("rows")
    core = lax.axis_index("clip")
    z, y = zy // YB, zy % YB
    me = x * YB + y
    up = ((z + ZB - 1) % ZB) * YB + y
    down = ((z + 1) % ZB) * YB + y

    def plane(i):
        t = (me + i) % 16
        return t, (t // YB, z * YB + t % YB, core)

    def start_lane(q):
        return pl.multiple_of(PADL + CH * (OWN * q - 4 + 2 * (q % 2)), 128)

    barrier = pltpu.get_barrier_semaphore()

    def greet(i, _):
        _, dev = plane(i)
        pl.semaphore_signal(barrier, inc=1, device_id=dev, device_id_type=MESH)
        return 0

    lax.fori_loop(1, 16, greet, 0)
    for dev in ((x, up, core), (x, down, core), (x, zy, 1 - core)):
        pl.semaphore_signal(barrier, inc=1, device_id=dev, device_id_type=MESH)
    pl.semaphore_wait(barrier, 18)

    def send_in(i):
        t, dev = plane(i)
        return pltpu.make_async_remote_copy(
            src_ref=feat.at[t // YB, :, pl.ds(start_lane(t % YB), WIN * CH)],
            dst_ref=arr.at[me],
            send_sem=s_a.at[t],
            recv_sem=r_a.at[me],
            device_id=dev,
            device_id_type=MESH,
        )

    def start_in(i, _):
        send_in(i).start()
        return 0

    lax.fori_loop(1, 16, start_in, 0)
    own_in = pltpu.make_async_copy(
        feat.at[x, :, pl.ds(start_lane(y), WIN * CH)], arr.at[me], l_sem
    )
    own_in.start()

    build_toeplitz(w1, wt1)
    build_toeplitz(w2, wt2)
    rw[...] = jnp.zeros_like(rw)

    def tap(i, _):
        rw[pl.ds(pl.multiple_of(128 * i, 128), CH), pl.ds(0, CH)] = wr[i]
        return 0

    lax.fori_loop(0, 9, tap, 0)

    own_in.wait()

    def wait_in(i, _):
        t, dev = plane(i)
        pltpu.make_async_remote_copy(
            src_ref=feat.at[0, :, pl.ds(0, WIN * CH)],
            dst_ref=arr.at[t],
            send_sem=s_a.at[t],
            recv_sem=r_a.at[t],
            device_id=dev,
            device_id_type=MESH,
        ).wait_recv()
        return 0

    lax.fori_loop(1, 16, wait_in, 0)

    gain1 = g1[...]
    gain2 = g2[...]
    lane8 = lane_iota((XB, 8, LANES))
    sub8 = lax.broadcasted_iota(jnp.int32, (8, LANES), 0)
    frame128 = lax.broadcasted_iota(jnp.int32, (128, LANES), 0) % 16

    def act_step(i, _):
        q, g = i // GROUPS, i % GROUPS
        lane0 = pl.multiple_of(g * 384, 128)
        v = [
            jnp.stack([arr[XB * xb + q, :, pl.ds(lane0 + 128 * m, 128)].astype(F32) for xb in range(XB)])
            for m in range(3)
        ]

        def rl(u, s):
            return pltpu.roll(u.reshape(XB * 8, LANES), s, 1).reshape(XB, 8, LANES)

        cols = [
            jnp.where(lane8 < 96, v[0], 0.0),
            jnp.where(lane8 < 32, rl(v[0], 32), jnp.where(lane8 < 96, rl(v[1], 32), 0.0)),
            jnp.where(lane8 < 64, rl(v[1], 64), jnp.where(lane8 < 96, rl(v[2], 64), 0.0)),
            jnp.where(lane8 < 96, rl(v[2], 96), 0.0),
        ]
        tiles = []
        for c in cols:
            turned = [pltpu.roll(c[xb], 4, 0) for xb in range(XB)]
            tiles += [jnp.where(sub8 < 4, c[0], turned[1]), jnp.where(sub8 < 4, c[2], turned[3])]
            tiles += [jnp.where(sub8 < 4, turned[0], c[1]), jnp.where(sub8 < 4, turned[2], c[3])]
        flat = jnp.concatenate(tiles, axis=0)
        w0 = 4 * g
        row = 2 * q
        xs[pl.ds(w0, 4), pl.ds(row, 2)] = flat.astype(BF16).reshape(4, 2, 16, LANES)
        act = norm_act(flat, gain1)
        for t in range(3):
            moved = act if t == 2 else shifted(act, 2 - t, frame128)
            a[t, pl.ds(w0, 4), pl.ds(row + 1, 2)] = moved.astype(BF16).reshape(4, 2, 16, LANES)
        return 0

    lax.fori_loop(0, YB * GROUPS, act_step, 0)

    def exchange(src_first, src_last, halo, k):
        copies = []
        if src_first is not None:
            copies.append(
                pltpu.make_async_remote_copy(
                    src_ref=src_first, dst_ref=halo.at[1], send_sem=s_z.at[k], recv_sem=r_z.at[k],
                    device_id=(x, up, core), device_id_type=MESH,
                )
            )
        if src_last is not None:
            copies.append(
                pltpu.make_async_remote_copy(
                    src_ref=src_last, dst_ref=halo.at[0], send_sem=s_z.at[k + 1], recv_sem=r_z.at[k + 1],
                    device_id=(x, down, core), device_id_type=MESH,
                )
            )
        for c in copies:
            c.start()
        return copies

    inside = (z > 0, z < ZB - 1)
    frame32 = lax.broadcasted_iota(jnp.int32, (32, LANES), 0) % 16

    def fill_halo(halo, dst, cols):
        def step(i, _):
            for side in range(2):
                v = halo[side, pl.ds(2 * i, 2)].astype(F32).reshape(32, LANES)
                v = jnp.where(inside[side], v, 0.0)
                for t in range(3):
                    moved = v if t == 2 else shifted(v, 2 - t, frame32)
                    dst[t, pl.ds(2 * i, 2), 9 * side] = moved.astype(BF16).reshape(2, 16, LANES)
            return 0

        lax.fori_loop(0, cols // 2, step, 0)

    copies = exchange(a.at[2, :, 1], a.at[2, :, 8], ha, 0)
    for c in copies:
        c.wait()
    fill_halo(ha, a, WIN)

    base = 2 * (1 - y % 2)
    col0 = OWN * y

    P1 = 3
    bias1 = b1[...]
    bias2 = b2[...]

    def conv1_step(i, _):
        acc = jnp.dot(conv_lhs(a, base, P1 * i, P1, 8), wt1[...].reshape(4608, 256), preferred_element_type=F32)
        for p in range(P1):
            for n in range(2):
                bcol = 2 * (P1 * i + p) + n
                v = acc[128 * p : 128 * p + 128, 128 * n : 128 * n + 128] + bias1
                act = norm_act(v, gain2)
                image = col0 - 1 + bcol
                act = jnp.where(jnp.logical_and(image >= 0, image < 104), act, 0.0)
                for t in range(3):
                    moved = act if t == 2 else shifted(act, 2 - t, frame128)
                    b[t, bcol, 1:9] = moved.astype(BF16).reshape(8, 16, LANES)
        return 0

    lax.fori_loop(0, PAIRS1 // P1, conv1_step, 0)

    copies = exchange(b.at[2, :, 1], b.at[2, :, 8], hb, 2)
    for c in copies:
        c.wait()
    fill_halo(hb, b, BC)

    P2 = 2

    def conv2_step(i, _):
        acc = jnp.dot(conv_lhs(b, 0, P2 * i, P2, 8), wt2[...].reshape(4608, 256), preferred_element_type=F32)
        for p in range(P2):
            for n in range(2):
                c = 2 * (P2 * i + p) + n
                v = acc[128 * p : 128 * p + 128, 128 * n : 128 * n + 128] + bias2
                v = v + xs[base + 2 + c].reshape(128, LANES).astype(F32)
                v = jnp.where(col0 + c < 104, v, 0.0)
                ob[c, 0:8] = v.astype(BF16).reshape(8, 16, LANES)
        return 0

    lax.fori_loop(0, PAIRS2 // P2, conv2_step, 0)

    copies = exchange(ob.at[:, 0], None, ho, 4)
    for c in copies:
        c.wait()

    def fill_last(c, _):
        ob[c, 8] = jnp.where(z < ZB - 1, ho[1, c].astype(F32), 0.0).astype(BF16)
        return 0

    lax.fori_loop(0, OC, fill_last, 0)

    bias_r = br[...]

    def reduce_step(jj, _):
        pieces = []
        for j2 in range(3):
            for k in range(3):
                rows = []
                for n in range(2):
                    c = jnp.minimum(4 * jj + 2 * n + k, OC - 1)
                    rows += [ob[c, 2 * i + j2] for i in range(4)]
                pieces.append(jnp.concatenate(rows, axis=0))
        acc = jnp.dot(jnp.concatenate(pieces, axis=1), rw[...], preferred_element_type=F32) + bias_r
        for i in range(4):
            for h in range(2):
                e = acc[16 * i + 8 * h : 16 * i + 8 * h + 8]
                o = acc[64 + 16 * i + 8 * h : 64 + 16 * i + 8 * h + 8]
                sb[2 * h, i, jj] = jnp.where(sub8 < 4, e, pltpu.roll(o, 4, 0)).astype(BF16)
                sb[2 * h + 1, i, jj] = jnp.where(sub8 < 4, pltpu.roll(e, 4, 0), o).astype(BF16)
        return 0

    lax.fori_loop(0, 7, reduce_step, 0)

    slot = XB * core + x

    def send_out(i):
        t, dev = plane(i)
        return pltpu.make_async_remote_copy(
            src_ref=sb.at[t // YB, t % YB],
            dst_ref=gb.at[slot, y],
            send_sem=s_g.at[t],
            recv_sem=r_g.at[me],
            device_id=dev,
            device_id_type=MESH,
        )

    def start_out(i, _):
        send_out(i).start()
        return 0

    lax.fori_loop(1, 16, start_out, 0)
    own_out = pltpu.make_async_copy(sb.at[x, y], gb.at[slot, y], l_sem)
    own_out.start()
    own_out.wait()

    def wait_out(i, _):
        t, dev = plane(i)
        pltpu.make_async_remote_copy(
            src_ref=sb.at[0, 0],
            dst_ref=gb.at[XB * core + t // YB, t % YB],
            send_sem=s_g.at[t],
            recv_sem=r_g.at[t],
            device_id=dev,
            device_id_type=MESH,
        ).wait_recv()
        return 0

    lax.fori_loop(1, 16, wait_out, 0)

    swap = pltpu.make_async_remote_copy(
        src_ref=gb.at[pl.ds(XB * core, XB)],
        dst_ref=gb.at[pl.ds(XB * core, XB)],
        send_sem=s_c,
        recv_sem=r_c,
        device_id=(x, zy, 1 - core),
        device_id_type=MESH,
    )
    swap.start()
    swap.wait()

    lane4 = lane_iota((8, LANES))
    for s in range(XB):
        src = jnp.int32(0)
        length = jnp.int32(0)
        for c in range(8):
            hit = owner[c] == XB * core + s
            src = jnp.where(hit, stored[c], src)
            length = jnp.where(hit, lengths[c], length)
        alive = (XB * x + sub8 % 4) < length

        for q in range(YB):
            tiles = gb[src, q]
            if q == 0:
                columns = []
            for j in range(JC):
                tile = tiles[j // 2].astype(F32)
                columns.append(tile if j % 2 == 0 else pltpu.roll(tile, 4, 0))
        for g in range(13):
            c0, c1, c2, c3 = columns[4 * g : 4 * g + 4]
            t1, t2, t3 = pltpu.roll(c1, 96, 1), pltpu.roll(c2, 64, 1), pltpu.roll(c3, 32, 1)
            dense = [jnp.where(lane4 < 96, c0, t1), jnp.where(lane4 < 64, t1, t2), jnp.where(lane4 < 32, t2, t3)]
            for m in range(3):
                out[s, :, pl.ds(384 * g + 128 * m, 128)] = jnp.where(alive, dense[m], 0.0)[0:4].astype(BF16)

    def end_sends(i, _):
        send_in(i).wait_send()
        send_out(i).wait_send()
        return 0

    lax.fori_loop(1, 16, end_sends, 0)


def local(
    features, lengths, stored_slot, owner_slot, gain_first, conv_first, bias_first,
    gain_second, conv_second, bias_second, reduce_conv_weight, reduce_conv_bias,
):
    slots, frames, rows, lanes = features.shape
    feat = jnp.transpose(features, (0, 2, 1, 3)).reshape(slots, rows * frames, lanes)
    feat = jnp.pad(feat, ((0, 0), (0, 0), (PADL, PADR)))

    def vec(v):
        return jnp.pad(v, (0, LANES - CH)).reshape(1, LANES)

    vmem = pl.BlockSpec(memory_space=pltpu.VMEM)
    smem = pl.BlockSpec(memory_space=pltpu.SMEM)
    result = pl.pallas_call(
        kernel,
        out_shape=jax.ShapeDtypeStruct((slots, frames, 4992), BF16),
        in_specs=[pl.BlockSpec(memory_space=pl.ANY)] + [vmem] * 8 + [smem] * 3,
        out_specs=vmem,
        scratch_shapes=[
            pltpu.VMEM((16, 8, WIN * CH), BF16),
            pltpu.VMEM((WIN, 8, 16, LANES), BF16),
            pltpu.VMEM((3, WIN, 10, 16, LANES), BF16),
            pltpu.VMEM((3, BC, 10, 16, LANES), BF16),
            pltpu.VMEM((9, 512, 256), BF16),
            pltpu.VMEM((9, 512, 256), BF16),
            pltpu.VMEM((1152, 128), BF16),
            pltpu.VMEM((OC, 9, 16, LANES), BF16),
            pltpu.VMEM((XB, 4, 7, 8, LANES), BF16),
            pltpu.VMEM((2 * XB, YB, 7, 8, LANES), BF16),
            pltpu.VMEM((2, WIN, 16, LANES), BF16),
            pltpu.VMEM((2, BC, 16, LANES), BF16),
            pltpu.VMEM((2, OC, 16, LANES), BF16),
            pltpu.SemaphoreType.DMA((16,)),
            pltpu.SemaphoreType.DMA((16,)),
            pltpu.SemaphoreType.DMA((6,)),
            pltpu.SemaphoreType.DMA((6,)),
            pltpu.SemaphoreType.DMA((16,)),
            pltpu.SemaphoreType.DMA((16,)),
            pltpu.SemaphoreType.DMA,
            pltpu.SemaphoreType.DMA,
            pltpu.SemaphoreType.DMA,
        ],
        compiler_params=pltpu.CompilerParams(
            collective_id=0, has_side_effects=True, vmem_limit_bytes=50 << 20
        ),
        name="encode",
    )(
        feat,
        conv_first.reshape(27, CH, CH),
        conv_second.reshape(27, CH, CH),
        reduce_conv_weight.reshape(9, CH, CH),
        vec(gain_first), vec(bias_first), vec(gain_second), vec(bias_second), vec(reduce_conv_bias),
        lengths, stored_slot, owner_slot,
    )
    return result.reshape(slots, frames, 1, 4992)


def solution(mesh):
    spec = P("clip", "tm", "rows", None)
    return jax.shard_map(
        local, mesh=mesh, in_specs=(spec,) + (P(),) * 11, out_specs=spec, check_vma=False
    )
```

```python
import jax
import jax.numpy as jnp
from jax import lax
from jax.experimental import pallas as pl
from jax.experimental.pallas import tpu as pltpu
from jax.sharding import PartitionSpec as P

NORM_EPS = 1e-06
MESH = pl.DeviceIdType.MESH
F32 = jnp.float32
BF16 = jnp.bfloat16

CH = 96
XB = 4
YB = 4
ZB = 8
OWN = 26
GROUPS = 9
WIN = GROUPS * 4
PADL = 384
PADR = 768
LANES = 128
PAIRS1 = 15
PAIRS2 = 14
BC = 2 * PAIRS1
OC = 2 * PAIRS2
JC = 13


def shifted(flat, step, frame):
    return jnp.where(frame < step, 0.0, pltpu.roll(flat, step, 0))


def silu(u):
    return 0.5 * u * (1.0 + jnp.tanh(0.5 * u))


def split_square(v):
    sq = v * v
    hi = sq.astype(BF16)
    return hi, (sq - hi.astype(F32)).astype(BF16)


def scaled_act(v, total, gain):
    return silu(v * lax.rsqrt(total * (1.0 / CH) + NORM_EPS) * gain)


def build_toeplitz(w_ref, wt):
    def tap(i, _):
        for n in range(2):
            for k in range(3):
                wt[i, pl.ds(128 * (n + k), CH), pl.ds(128 * n, CH)] = w_ref[3 * i + k]
        return 0

    lax.fori_loop(0, 9, tap, 0)


def conv_lhs(src, col0, pairs, rows):
    parts = []
    for t in range(3):
        for j in range(3):
            for k in range(4):
                pieces = []
                for p in range(pairs):
                    for first, count in rows:
                        block = src[t, col0 + 2 * p + k, first + j : first + j + count]
                        pieces.append(block.reshape(count * 16, LANES))
                parts.append(jnp.concatenate(pieces, axis=0))
    return jnp.concatenate(parts, axis=1)


INNER = ((1, 6),)
EDGES = ((0, 1), (7, 1))


def kernel(
    feat, w1h, w2h, wrh, g1h, b1h, g2h, b2h, brh, lenh, stoh, ownh, out,
    arr, xs, a, b, wt1, wt2, rw, ob, sb, gb, ha, hb, ho, w1, w2, wr, vin, vec, ones2,
    lengths, stored, owner,
    s_a, r_a, s_z, r_z, s_g, r_g, l_a, l_w,
):
    x = lax.axis_index("tm")
    zy = lax.axis_index("rows")
    core = lax.axis_index("clip")
    z, y = zy // YB, zy % YB
    me = x * YB + y
    up = ((z + ZB - 1) % ZB) * YB + y
    down = ((z + 1) % ZB) * YB + y

    def plane(i):
        t = (me + i) % 16
        return t, (t // YB, z * YB + t % YB, core)

    def start_lane(q):
        return pl.multiple_of(PADL + CH * (OWN * q - 4 + 2 * (q % 2)), 128)

    arr[:, :, 0:128] = jnp.zeros((16, 8, 128), BF16)
    arr[:, :, 3072:3456] = jnp.zeros((16, 8, 384), BF16)
    barrier = pltpu.get_barrier_semaphore()

    def greet(i, _):
        t = (me + i) % 16
        c = (core + i // 16) % 2
        pl.semaphore_signal(
            barrier, inc=1, device_id=(t // YB, z * YB + t % YB, c), device_id_type=MESH
        )
        return 0

    lax.fori_loop(1, 32, greet, 0)
    for row in (up, down):
        pl.semaphore_signal(barrier, inc=1, device_id=(x, row, core), device_id_type=MESH)

    loads = [
        pltpu.make_async_copy(src, dst, l_w.at[i])
        for i, (src, dst) in enumerate(
            [(w1h, w1), (w2h, w2), (wrh, wr)]
            + [(v, vin.at[i]) for i, v in enumerate((g1h, b1h, g2h, b2h, brh))]
            + [(lenh, lengths), (stoh, stored), (ownh, owner)]
        )
    ]
    for c in loads:
        c.start()

    def zero_weights(i, _):
        wt1[i] = jnp.zeros((512, 256), BF16)
        wt2[i] = jnp.zeros((512, 256), BF16)
        return 0

    lax.fori_loop(0, 9, zero_weights, 0)
    rw[...] = jnp.zeros_like(rw)
    vec[...] = jnp.zeros_like(vec)
    r_i = lax.broadcasted_iota(jnp.int32, (256, 256), 0) // 128
    c_i = lax.broadcasted_iota(jnp.int32, (256, 256), 1) // 128
    ones2[...] = jnp.where(r_i == c_i, 1.0, 0.0).astype(BF16)
    loads[0].wait()
    build_toeplitz(w1, wt1)
    pl.semaphore_wait(barrier, 33)

    HALF = 1536
    odd = y % 2

    def in_copy(i, chunk):
        t, dev = plane(i)
        q = t % YB
        off = 128 * (1 - q % 2) + HALF * chunk
        src = feat.at[t // YB, :, pl.ds(pl.multiple_of(start_lane(q) + off, 128), HALF)]
        dst = arr.at[me, :, pl.ds(pl.multiple_of(off, 128), HALF)]
        return pltpu.make_async_remote_copy(
            src_ref=src, dst_ref=dst, send_sem=s_a.at[chunk, t], recv_sem=r_a.at[chunk, me],
            device_id=dev, device_id_type=MESH,
        )

    my_off = 128 * (1 - odd)
    own_in = pltpu.make_async_copy(
        feat.at[x, :, pl.ds(pl.multiple_of(start_lane(y) + my_off, 128), 2 * HALF)],
        arr.at[me, :, pl.ds(pl.multiple_of(my_off, 128), 2 * HALF)],
        l_a.at[0],
    )
    own_in.start()
    for chunk in range(2):

        def start_in(i, _):
            in_copy(i, chunk).start()
            return 0

        lax.fori_loop(1, 16, start_in, 0)

    for c in loads[1:]:
        c.wait()
    build_toeplitz(w2, wt2)

    def tap(i, _):
        rw[pl.ds(pl.multiple_of(128 * i, 128), CH), pl.ds(0, CH)] = wr[i]
        return 0

    lax.fori_loop(0, 9, tap, 0)
    for i in range(5):
        vec[i : i + 1, 0:CH] = vin[i]
    gain1, bias1, gain2, bias2, bias_r = [vec[i : i + 1] for i in range(5)]
    bias1w = jnp.concatenate([bias1, bias1], axis=1)
    gain2w = jnp.concatenate([gain2, gain2], axis=1)
    bias2w = jnp.concatenate([bias2, bias2], axis=1)

    own_in.wait()

    def wait_in(chunk):
        def step(i, _):
            t, dev = plane(i)
            dst = arr.at[t, :, pl.ds(pl.multiple_of(my_off + HALF * chunk, 128), HALF)]
            pltpu.make_async_remote_copy(
                src_ref=feat.at[0, :, pl.ds(0, HALF)], dst_ref=dst,
                send_sem=s_a.at[chunk, t], recv_sem=r_a.at[chunk, t],
                device_id=dev, device_id_type=MESH,
            ).wait_recv()
            return 0

        lax.fori_loop(1, 16, step, 0)

    lane = lax.broadcasted_iota(jnp.int32, (8, LANES), 1)
    sub8 = lax.broadcasted_iota(jnp.int32, (8, LANES), 0)
    frame128 = lax.broadcasted_iota(jnp.int32, (128, LANES), 0) % 16
    ones1 = jnp.ones((256, 128), BF16)

    def act_group(q, g):
        lane0 = pl.multiple_of(g * 384, 128)
        cols = [[] for _ in range(4)]
        for xb in range(XB):
            v = [arr[XB * xb + q, :, pl.ds(lane0 + 128 * m, 128)].astype(F32) for m in range(3)]
            cols[0].append(jnp.where(lane < 96, v[0], 0.0))
            cols[1].append(
                jnp.where(lane < 32, pltpu.roll(v[0], 32, 1), jnp.where(lane < 96, pltpu.roll(v[1], 32, 1), 0.0))
            )
            cols[2].append(
                jnp.where(lane < 64, pltpu.roll(v[1], 64, 1), jnp.where(lane < 96, pltpu.roll(v[2], 64, 1), 0.0))
            )
            cols[3].append(jnp.where(lane < 96, pltpu.roll(v[2], 96, 1), 0.0))
        tiles = []
        for c in cols:
            turned = [pltpu.roll(u, 4, 0) for u in c]
            tiles += [jnp.where(sub8 < 4, c[0], turned[1]), jnp.where(sub8 < 4, c[2], turned[3])]
            tiles += [jnp.where(sub8 < 4, turned[0], c[1]), jnp.where(sub8 < 4, turned[2], c[3])]
        return jnp.concatenate(tiles, axis=0)

    def act_store(flat, total, q, g):
        w0 = 4 * g
        row = 2 * q
        xs[pl.ds(w0, 4), pl.ds(row, 2)] = flat.astype(BF16).reshape(4, 2, 16, LANES)
        act = scaled_act(flat, total, gain1)
        for t in range(3):
            moved = act if t == 2 else shifted(act, 2 - t, frame128)
            a[t, pl.ds(w0, 4), pl.ds(row + 1, 2)] = moved.astype(BF16).reshape(4, 2, 16, LANES)

    def act_step(i, qs):
        flats = [act_group(q, i) for q in qs]
        hi, lo = split_square(jnp.concatenate(flats, axis=0))
        total = jnp.dot(jnp.concatenate([hi, lo], axis=1), ones1, preferred_element_type=F32)
        for m, q in enumerate(qs):
            act_store(flats[m], total[128 * m : 128 * m + 128], q, i)
        return 0

    def z_copy(src, dst, k, row):
        return pltpu.make_async_remote_copy(
            src_ref=src, dst_ref=dst, send_sem=s_z.at[k], recv_sem=r_z.at[k],
            device_id=(x, row, core), device_id_type=MESH,
        )

    inside = (z > 0, z < ZB - 1)

    def fill_halo(halo, dst, first, count, unit):
        frame = lax.broadcasted_iota(jnp.int32, (16 * unit, LANES), 0) % 16

        def step(i, _):
            c = first + unit * i
            for side in range(2):
                v = halo[side, pl.ds(c, unit)].astype(F32).reshape(16 * unit, LANES)
                v = jnp.where(inside[side], v, 0.0)
                for t in range(3):
                    moved = v if t == 2 else shifted(v, 2 - t, frame)
                    dst[t, pl.ds(c, unit), 9 * side] = moved.astype(BF16).reshape(unit, 16, LANES)
            return 0

        lax.fori_loop(0, count // unit, step, 0)

    base = 2 * (1 - odd)
    col0 = OWN * y

    def conv1(p0, pairs, rows):
        acc = jnp.dot(
            conv_lhs(a, base + 2 * p0, pairs, rows), wt1[...].reshape(4608, 256), preferred_element_type=F32
        )
        v = acc + bias1w
        hi, lo = split_square(v)
        total = jnp.dot(hi, ones2[...], preferred_element_type=F32) + jnp.dot(
            lo, ones2[...], preferred_element_type=F32
        )
        act = scaled_act(v, total, gain2w)
        height = sum(count for _, count in rows)
        m = 16 * height
        frame = lax.broadcasted_iota(jnp.int32, (m, LANES), 0) % 16
        for p in range(pairs):
            for n in range(2):
                bcol = 2 * (p0 + p) + n
                image = col0 - 1 + bcol
                u = act[m * p : m * p + m, 128 * n : 128 * n + 128]
                u = jnp.where(jnp.logical_and(image >= 0, image < 104), u, 0.0)
                for t in range(3):
                    moved = (u if t == 2 else shifted(u, 2 - t, frame)).astype(BF16)
                    at = 0
                    for first, count in rows:
                        b[t, bcol, first + 1 : first + 1 + count] = moved[16 * at : 16 * (at + count)].reshape(
                            count, 16, LANES
                        )
                        at += count

    def conv2(p0, pairs, rows):
        acc = jnp.dot(
            conv_lhs(b, 2 * p0, pairs, rows), wt2[...].reshape(4608, 256), preferred_element_type=F32
        )
        v = acc + bias2w
        height = sum(count for _, count in rows)
        m = 16 * height
        for p in range(pairs):
            for n in range(2):
                c = 2 * (p0 + p) + n
                u = v[m * p : m * p + m, 128 * n : 128 * n + 128]
                at = 0
                for first, count in rows:
                    part = u[16 * at : 16 * (at + count)]
                    part = part + xs[base + 2 + c, first : first + count].reshape(16 * count, LANES).astype(F32)
                    part = jnp.where(col0 + c < 104, part, 0.0)
                    ob[c, first : first + count] = part.astype(BF16).reshape(count, 16, LANES)
                    at += count

    CUT = (0, 16, 36)
    sends_a = []
    for chunk in range(2):
        wait_in(chunk)
        lo_w, hi_w = CUT[chunk], CUT[chunk + 1]
        lax.fori_loop(lo_w // 4, hi_w // 4, lambda i, _: act_step(i, (0, 3)), 0)
        part = pl.ds(lo_w, hi_w - lo_w)
        sends_a += [
            z_copy(a.at[2, part, 1], ha.at[1, part], 2 * chunk, up),
            z_copy(a.at[2, part, 8], ha.at[0, part], 2 * chunk + 1, down),
        ]
        sends_a[-2].start()
        sends_a[-1].start()
        lax.fori_loop(lo_w // 4, hi_w // 4, lambda i, _: act_step(i, (1, 2)), 0)

        def inner1(i, _):
            conv1(3 * i, 3, INNER)
            return 0

        lax.fori_loop(2 * chunk, 2 + 3 * chunk, inner1, 0)
    for c in sends_a:
        c.wait()
    fill_halo(ha, a, 0, WIN, 4)

    def edge1(i, _):
        conv1(5 * i, 5, EDGES)
        return 0

    lax.fori_loop(0, 3, edge1, 0)
    sends_b = [z_copy(b.at[2, :, 1], hb.at[1], 4, up), z_copy(b.at[2, :, 8], hb.at[0], 5, down)]
    for c in sends_b:
        c.start()

    def inner2(i, _):
        conv2(7 * i, 7, INNER)
        return 0

    lax.fori_loop(0, 2, inner2, 0)
    for c in sends_b:
        c.wait()
    fill_halo(hb, b, 0, BC, 5)
    conv2(0, PAIRS2, ((0, 1),))
    send_o = z_copy(ob.at[:, 0], ho, 6, up)
    send_o.start()
    conv2(0, PAIRS2, ((7, 1),))

    def reduce_rows(rows):
        pieces = []
        for j2 in range(3):
            for k in range(3):
                tiles = []
                for j in range(14):
                    c = min(2 * j + k, OC - 1)
                    tiles += [ob[c, 2 * i + j2] for i in rows]
                pieces.append(jnp.concatenate(tiles, axis=0))
        acc = jnp.dot(jnp.concatenate(pieces, axis=1), rw[...], preferred_element_type=F32) + bias_r
        m = 16 * len(rows)
        for n, i in enumerate(rows):
            for jj in range(7):
                for h in range(2):
                    at = 2 * jj * m + 16 * n + 8 * h
                    e, o = acc[at : at + 8], acc[at + m : at + m + 8]
                    sb[2 * h, i, jj] = jnp.where(sub8 < 4, e, pltpu.roll(o, 4, 0)).astype(BF16)
                    sb[2 * h + 1, i, jj] = jnp.where(sub8 < 4, pltpu.roll(e, 4, 0), o).astype(BF16)

    slot = XB * core + x

    def out_copy(i, k):
        xb = (x + k // 2) % XB
        c = (core + k) % 2
        return pltpu.make_async_remote_copy(
            src_ref=sb.at[xb, i], dst_ref=gb.at[slot, y], send_sem=s_g.at[i, k], recv_sem=r_g.at[slot, y],
            device_id=(xb, z * YB + i, c), device_id_type=MESH,
        )

    def start_out(i):
        def step(k, _):
            here = jnp.logical_and(k == 0, y == i)

            @pl.when(jnp.logical_not(here))
            def _():
                out_copy(i, k).start()

            return 0

        lax.fori_loop(0, 8, step, 0)

    reduce_rows((0, 1, 2))
    for i in range(3):
        start_out(i)
    send_o.wait()

    def fill_last(i, _):
        v = ho[pl.ds(7 * i, 7)].astype(F32)
        ob[pl.ds(7 * i, 7), 8] = jnp.where(z < ZB - 1, v, 0.0).astype(BF16)
        return 0

    lax.fori_loop(0, 4, fill_last, 0)
    reduce_rows((3,))
    start_out(3)
    own_out = pltpu.make_async_copy(sb.at[x, y], gb.at[slot, y], l_a.at[1])
    own_out.start()
    own_out.wait()

    def wait_out(k, _):
        s, q = k // YB, k % YB

        @pl.when(jnp.logical_not(jnp.logical_and(s == slot, q == y)))
        def _():
            pltpu.make_async_remote_copy(
                src_ref=sb.at[0, 0], dst_ref=gb.at[s, q], send_sem=s_g.at[0, 0], recv_sem=r_g.at[s, q],
                device_id=(x, zy, 1 - core), device_id_type=MESH,
            ).wait_recv()

        return 0

    lax.fori_loop(0, 32, wait_out, 0)

    def select(s, _):
        src = jnp.int32(0)
        length = jnp.int32(0)
        for c in range(8):
            hit = owner[c] == XB * core + s
            src = jnp.where(hit, stored[c], src)
            length = jnp.where(hit, lengths[c], length)
        alive = (XB * x + sub8 % 4) < length
        columns = []
        for q in range(YB):
            tiles = gb[src, q]
            for j in range(JC):
                tile = tiles[j // 2].astype(F32)
                columns.append(tile if j % 2 == 0 else pltpu.roll(tile, 4, 0))
        for g in range(13):
            c0, c1, c2, c3 = columns[4 * g : 4 * g + 4]
            t1, t2, t3 = pltpu.roll(c1, 96, 1), pltpu.roll(c2, 64, 1), pltpu.roll(c3, 32, 1)
            dense = [jnp.where(lane < 96, c0, t1), jnp.where(lane < 64, t1, t2), jnp.where(lane < 32, t2, t3)]
            for m in range(3):
                out[s, :, pl.ds(384 * g + 128 * m, 128)] = jnp.where(alive, dense[m], 0.0)[0:4].astype(BF16)
        return 0

    lax.fori_loop(0, XB, select, 0)

    def end_in(i, _):
        in_copy(i, 0).wait_send()
        in_copy(i, 1).wait_send()
        return 0

    lax.fori_loop(1, 16, end_in, 0)

    def end_out(k, _):
        for i in range(4):

            @pl.when(jnp.logical_not(jnp.logical_and(k == 0, y == i)))
            def _():
                out_copy(i, k).wait_send()

        return 0

    lax.fori_loop(0, 8, end_out, 0)


def local(
    features, lengths, stored_slot, owner_slot, gain_first, conv_first, bias_first,
    gain_second, conv_second, bias_second, reduce_conv_weight, reduce_conv_bias,
):
    slots, frames, rows, lanes = features.shape
    feat = jnp.transpose(features, (0, 2, 1, 3)).reshape(slots, rows * frames, lanes)
    feat = jnp.pad(feat, ((0, 0), (0, 0), (PADL, PADR)))
    hbm = pl.BlockSpec(memory_space=pltpu.HBM)
    dma = pltpu.SemaphoreType.DMA
    result = pl.pallas_call(
        kernel,
        out_shape=jax.ShapeDtypeStruct((slots, frames, 4992), BF16),
        in_specs=[pl.BlockSpec(memory_space=pl.ANY)] + [hbm] * 11,
        out_specs=pl.BlockSpec(memory_space=pltpu.VMEM),
        scratch_shapes=[
            pltpu.VMEM((16, 8, WIN * CH), BF16),
            pltpu.VMEM((WIN, 8, 16, LANES), BF16),
            pltpu.VMEM((3, WIN, 10, 16, LANES), BF16),
            pltpu.VMEM((3, BC, 10, 16, LANES), BF16),
            pltpu.VMEM((9, 512, 256), BF16),
            pltpu.VMEM((9, 512, 256), BF16),
            pltpu.VMEM((1152, 128), BF16),
            pltpu.VMEM((OC, 9, 16, LANES), BF16),
            pltpu.VMEM((XB, 4, 7, 8, LANES), BF16),
            pltpu.VMEM((2 * XB, YB, 7, 8, LANES), BF16),
            pltpu.VMEM((2, WIN, 16, LANES), BF16),
            pltpu.VMEM((2, BC, 16, LANES), BF16),
            pltpu.VMEM((OC, 16, LANES), BF16),
            pltpu.VMEM((27, CH, CH), BF16),
            pltpu.VMEM((27, CH, CH), BF16),
            pltpu.VMEM((9, CH, CH), BF16),
            pltpu.VMEM((5, 1, CH), F32),
            pltpu.VMEM((8, LANES), F32),
            pltpu.VMEM((256, 256), BF16),
            pltpu.SMEM((8,), jnp.int32),
            pltpu.SMEM((8,), jnp.int32),
            pltpu.SMEM((8,), jnp.int32),
            dma((2, 16)),
            dma((2, 16)),
            dma((7,)),
            dma((7,)),
            dma((4, 8)),
            dma((8, 4)),
            dma((2,)),
            dma((11,)),
        ],
        compiler_params=pltpu.CompilerParams(
            collective_id=0, has_side_effects=True, vmem_limit_bytes=50 << 20
        ),
        name="encode",
    )(
        feat,
        conv_first.reshape(27, CH, CH),
        conv_second.reshape(27, CH, CH),
        reduce_conv_weight.reshape(9, CH, CH),
        *[v.reshape(1, CH) for v in (gain_first, bias_first, gain_second, bias_second, reduce_conv_bias)],
        lengths, stored_slot, owner_slot,
    )
    return result.reshape(slots, frames, 1, 4992)


def solution(mesh):
    spec = P("clip", "tm", "rows", None)
    return jax.shard_map(
        local, mesh=mesh, in_specs=(spec,) + (P(),) * 11, out_specs=spec, check_vma=False
    )
```

```python
import jax
import jax.numpy as jnp
from jax import lax
from jax.experimental import pallas as pl
from jax.experimental.pallas import tpu as pltpu
from jax.sharding import PartitionSpec as P

NORM_EPS = 1e-06
MESH = pl.DeviceIdType.MESH
F32 = jnp.float32
BF16 = jnp.bfloat16

CH = 96
XB = 4
YB = 4
ZB = 8
OWN = 26
GROUPS = 9
WIN = GROUPS * 4
PADL = 384
PADR = 768
LANES = 128
PAIRS1 = 15
PAIRS2 = 14
BC = 2 * PAIRS1
OC = 2 * PAIRS2
JC = 13


def shifted(flat, step, frame):
    return jnp.where(frame < step, 0.0, pltpu.roll(flat, step, 0))


def square(v):
    return (v * v).astype(BF16)


def scaled_act(v, total, half_gain):
    half = v * lax.rsqrt(total * (1.0 / CH) + NORM_EPS) * half_gain
    return half + half * jnp.tanh(half)


def build_toeplitz(w_ref, wt):
    def tap(i, _):
        for n in range(2):
            for k in range(3):
                wt[i, pl.ds(128 * (n + k), CH), pl.ds(128 * n, CH)] = w_ref[3 * i + k]
        return 0

    lax.fori_loop(0, 9, tap, 0)


def conv_lhs(src, col0, pairs, rows):
    parts = []
    for t in range(3):
        for j in range(3):
            for k in range(4):
                pieces = []
                for p in range(pairs):
                    for first, count in rows:
                        block = src[t, col0 + 2 * p + k, first + j : first + j + count]
                        pieces.append(block.reshape(count * 16, LANES))
                parts.append(jnp.concatenate(pieces, axis=0))
    return jnp.concatenate(parts, axis=1)


INNER = ((1, 6),)
EDGES = ((0, 1), (7, 1))


def kernel(
    feat, w1h, w2h, wrh, g1h, b1h, g2h, b2h, brh, lenh, stoh, ownh, out,
    arr, xs, a, b, wt1, wt2, rw, ob, sb, gb, ha, hb, ho, w1, w2, wr, vin, vec, ones2,
    lengths, stored, owner,
    s_a, r_a, s_z, r_z, s_g, r_g, l_a, l_w,
):
    x = lax.axis_index("tm")
    zy = lax.axis_index("rows")
    core = lax.axis_index("clip")
    z, y = zy // YB, zy % YB
    me = x * YB + y
    up = ((z + ZB - 1) % ZB) * YB + y
    down = ((z + 1) % ZB) * YB + y

    def plane(i):
        t = (me + i) % 16
        return t, (t // YB, z * YB + t % YB, core)

    def start_lane(q):
        return pl.multiple_of(PADL + CH * (OWN * q - 4 + 2 * (q % 2)), 128)

    arr[:, :, 0:128] = jnp.zeros((16, 8, 128), BF16)
    arr[:, :, 3072:3456] = jnp.zeros((16, 8, 384), BF16)
    barrier = pltpu.get_barrier_semaphore()

    xs_of = [(x + d) % XB for d in range(XB)]
    ys_of = [(y + d) % YB for d in range(YB)]
    for dx in range(XB):
        for dy in range(YB):
            if dx or dy:
                dev = (xs_of[dx], z * YB + ys_of[dy], core)
                pl.semaphore_signal(barrier, inc=1, device_id=dev, device_id_type=MESH)
    for dev in ((x, up, core), (x, down, core), (x, zy, 1 - core)):
        pl.semaphore_signal(barrier, inc=1, device_id=dev, device_id_type=MESH)

    loads = [
        pltpu.make_async_copy(src, dst, l_w.at[i])
        for i, (src, dst) in enumerate(
            [(w1h, w1), (w2h, w2), (wrh, wr)]
            + [(v, vin.at[i]) for i, v in enumerate((g1h, b1h, g2h, b2h, brh))]
            + [(lenh, lengths), (stoh, stored), (ownh, owner)]
        )
    ]
    for c in loads:
        c.start()

    def zero_weights(i, _):
        wt1[i] = jnp.zeros((512, 256), BF16)
        wt2[i] = jnp.zeros((512, 256), BF16)
        return 0

    lax.fori_loop(0, 9, zero_weights, 0)
    rw[...] = jnp.zeros_like(rw)
    vec[...] = jnp.zeros_like(vec)
    r_i = lax.broadcasted_iota(jnp.int32, (256, 256), 0) // 128
    c_i = lax.broadcasted_iota(jnp.int32, (256, 256), 1) // 128
    ones2[...] = jnp.where(r_i == c_i, 1.0, 0.0).astype(BF16)
    loads[0].wait()
    build_toeplitz(w1, wt1)
    pl.semaphore_wait(barrier, 18)

    HALF = 1024
    odd = y % 2

    def in_copy(i, chunk):
        t, dev = plane(i)
        q = t % YB
        off = 128 * (1 - q % 2) + HALF * chunk
        src = feat.at[t // YB, :, pl.ds(pl.multiple_of(start_lane(q) + off, 128), HALF)]
        dst = arr.at[me, :, pl.ds(pl.multiple_of(off, 128), HALF)]
        return pltpu.make_async_remote_copy(
            src_ref=src, dst_ref=dst, send_sem=s_a.at[chunk, t], recv_sem=r_a.at[chunk, me],
            device_id=dev, device_id_type=MESH,
        )

    my_off = 128 * (1 - odd)
    own_in = pltpu.make_async_copy(
        feat.at[x, :, pl.ds(pl.multiple_of(start_lane(y) + my_off, 128), 3 * HALF)],
        arr.at[me, :, pl.ds(pl.multiple_of(my_off, 128), 3 * HALF)],
        l_a.at[0],
    )
    own_in.start()
    for chunk in range(3):

        def start_in(i, _):
            in_copy(i, chunk).start()
            return 0

        lax.fori_loop(1, 16, start_in, 0)

    for c in loads[1:]:
        c.wait()
    build_toeplitz(w2, wt2)

    def tap(i, _):
        rw[pl.ds(pl.multiple_of(128 * i, 128), CH), pl.ds(0, CH)] = wr[i]
        return 0

    lax.fori_loop(0, 9, tap, 0)
    for i in range(5):
        vec[i : i + 1, 0:CH] = vin[i]
    gain1, bias1, gain2, bias2, bias_r = [vec[i : i + 1] for i in range(5)]
    gain1, gain2 = 0.5 * gain1, 0.5 * gain2
    bias1w = jnp.concatenate([bias1, bias1], axis=1)
    gain2w = jnp.concatenate([gain2, gain2], axis=1)
    bias2w = jnp.concatenate([bias2, bias2], axis=1)

    own_in.wait()

    def wait_in(chunk):
        def step(i, _):
            t, dev = plane(i)
            dst = arr.at[t, :, pl.ds(pl.multiple_of(my_off + HALF * chunk, 128), HALF)]
            pltpu.make_async_remote_copy(
                src_ref=feat.at[0, :, pl.ds(0, HALF)], dst_ref=dst,
                send_sem=s_a.at[chunk, t], recv_sem=r_a.at[chunk, t],
                device_id=dev, device_id_type=MESH,
            ).wait_recv()
            return 0

        lax.fori_loop(1, 16, step, 0)

    lane = lax.broadcasted_iota(jnp.int32, (8, LANES), 1)
    sub8 = lax.broadcasted_iota(jnp.int32, (8, LANES), 0)
    frame128 = lax.broadcasted_iota(jnp.int32, (128, LANES), 0) % 16

    def act_group(q, g):
        lane0 = pl.multiple_of(g * 384, 128)
        cols = [[] for _ in range(4)]
        for xb in range(XB):
            v = [arr[XB * xb + q, :, pl.ds(lane0 + 128 * m, 128)].astype(F32) for m in range(3)]
            cols[0].append(jnp.where(lane < 96, v[0], 0.0))
            cols[1].append(
                jnp.where(lane < 32, pltpu.roll(v[0], 32, 1), jnp.where(lane < 96, pltpu.roll(v[1], 32, 1), 0.0))
            )
            cols[2].append(
                jnp.where(lane < 64, pltpu.roll(v[1], 64, 1), jnp.where(lane < 96, pltpu.roll(v[2], 64, 1), 0.0))
            )
            cols[3].append(jnp.where(lane < 96, pltpu.roll(v[2], 96, 1), 0.0))
        tiles = []
        for c in cols:
            turned = [pltpu.roll(u, 4, 0) for u in c]
            tiles += [jnp.where(sub8 < 4, c[0], turned[1]), jnp.where(sub8 < 4, c[2], turned[3])]
            tiles += [jnp.where(sub8 < 4, turned[0], c[1]), jnp.where(sub8 < 4, turned[2], c[3])]
        return jnp.concatenate(tiles, axis=0)

    def act_store(flat, total, q, g):
        w0 = 4 * g
        row = 2 * q
        xs[pl.ds(w0, 4), pl.ds(row, 2)] = flat.astype(BF16).reshape(4, 2, 16, LANES)
        act = scaled_act(flat, total, gain1)
        for t in range(3):
            moved = act if t == 2 else shifted(act, 2 - t, frame128)
            a[t, pl.ds(w0, 4), pl.ds(row + 1, 2)] = moved.astype(BF16).reshape(4, 2, 16, LANES)

    def act_step(i, qs):
        flats = [act_group(q, i) for q in qs]
        both = jnp.concatenate([square(u) for u in flats], axis=1)
        total = jnp.dot(both, ones2[...], preferred_element_type=F32)
        for m, q in enumerate(qs):
            act_store(flats[m], total[:, 128 * m : 128 * m + 128], q, i)
        return 0

    def z_copy(src, dst, k, row):
        return pltpu.make_async_remote_copy(
            src_ref=src, dst_ref=dst, send_sem=s_z.at[k], recv_sem=r_z.at[k],
            device_id=(x, row, core), device_id_type=MESH,
        )

    inside = (z > 0, z < ZB - 1)

    def fill_halo(halo, dst, first, count, unit):
        frame = lax.broadcasted_iota(jnp.int32, (16 * unit, LANES), 0) % 16

        def step(i, _):
            c = first + unit * i
            for side in range(2):
                v = halo[side, pl.ds(c, unit)].astype(F32).reshape(16 * unit, LANES)
                v = jnp.where(inside[side], v, 0.0)
                for t in range(3):
                    moved = v if t == 2 else shifted(v, 2 - t, frame)
                    dst[t, pl.ds(c, unit), 9 * side] = moved.astype(BF16).reshape(unit, 16, LANES)
            return 0

        lax.fori_loop(0, count // unit, step, 0)

    base = 2 * (1 - odd)
    col0 = OWN * y

    def conv1(p0, pairs, rows):
        acc = jnp.dot(
            conv_lhs(a, base + 2 * p0, pairs, rows), wt1[...].reshape(4608, 256), preferred_element_type=F32
        )
        v = acc + bias1w
        total = jnp.dot(square(v), ones2[...], preferred_element_type=F32)
        act = scaled_act(v, total, gain2w)
        height = sum(count for _, count in rows)
        m = 16 * height
        frame = lax.broadcasted_iota(jnp.int32, (m, LANES), 0) % 16
        for p in range(pairs):
            for n in range(2):
                bcol = 2 * (p0 + p) + n
                image = col0 - 1 + bcol
                u = act[m * p : m * p + m, 128 * n : 128 * n + 128]
                u = jnp.where(jnp.logical_and(image >= 0, image < 104), u, 0.0)
                for t in range(3):
                    moved = (u if t == 2 else shifted(u, 2 - t, frame)).astype(BF16)
                    at = 0
                    for first, count in rows:
                        b[t, bcol, first + 1 : first + 1 + count] = moved[16 * at : 16 * (at + count)].reshape(
                            count, 16, LANES
                        )
                        at += count

    def conv2(p0, pairs, rows):
        acc = jnp.dot(
            conv_lhs(b, 2 * p0, pairs, rows), wt2[...].reshape(4608, 256), preferred_element_type=F32
        )
        v = acc + bias2w
        height = sum(count for _, count in rows)
        m = 16 * height
        for p in range(pairs):
            for n in range(2):
                c = 2 * (p0 + p) + n
                u = v[m * p : m * p + m, 128 * n : 128 * n + 128]
                at = 0
                for first, count in rows:
                    part = u[16 * at : 16 * (at + count)]
                    part = part + xs[base + 2 + c, first : first + count].reshape(16 * count, LANES).astype(F32)
                    part = jnp.where(col0 + c < 104, part, 0.0)
                    ob[c, first : first + count] = part.astype(BF16).reshape(count, 16, LANES)
                    at += count

    CUT = (0, 8, 20, 36)
    INNER_CUT = (0, 0, 2, 5)

    def inner1(i, _):
        conv1(3 * i, 3, INNER)
        return 0

    sends_a = []
    for chunk in range(3):
        wait_in(chunk)
        lo_w, hi_w = CUT[chunk], CUT[chunk + 1]
        lax.fori_loop(lo_w // 4, hi_w // 4, lambda i, _: act_step(i, (0, 3)), 0)
        part = pl.ds(lo_w, hi_w - lo_w)
        sends_a += [
            z_copy(a.at[2, part, 1], ha.at[1, part], 2 * chunk, up),
            z_copy(a.at[2, part, 8], ha.at[0, part], 2 * chunk + 1, down),
        ]
        sends_a[-2].start()
        sends_a[-1].start()
        lax.fori_loop(lo_w // 4, hi_w // 4, lambda i, _: act_step(i, (1, 2)), 0)
        if INNER_CUT[chunk] < INNER_CUT[chunk + 1]:
            lax.fori_loop(INNER_CUT[chunk], INNER_CUT[chunk + 1], inner1, 0)
    for c in sends_a:
        c.wait()
    fill_halo(ha, a, 0, WIN, 4)

    sends_b = []
    for e in range(3):
        conv1(5 * e, 5, EDGES)
        part = pl.ds(10 * e, 10)
        sends_b += [
            z_copy(b.at[2, part, 1], hb.at[1, part], 6 + 2 * e, up),
            z_copy(b.at[2, part, 8], hb.at[0, part], 7 + 2 * e, down),
        ]
        sends_b[-2].start()
        sends_b[-1].start()

    conv2(0, 7, INNER)
    for c in sends_b:
        c.wait()
    fill_halo(hb, b, 0, BC, 5)
    conv2(0, PAIRS2, ((0, 1),))
    send_o = z_copy(ob.at[:, 0], ho, 12, up)
    send_o.start()
    conv2(7, 7, INNER)

    def reduce_rows(rows):
        pieces = []
        for j2 in range(3):
            for k in range(3):
                tiles = []
                for j in range(14):
                    c = min(2 * j + k, OC - 1)
                    tiles += [ob[c, 2 * i + j2] for i in rows]
                pieces.append(jnp.concatenate(tiles, axis=0))
        acc = jnp.dot(jnp.concatenate(pieces, axis=1), rw[...], preferred_element_type=F32) + bias_r
        m = 16 * len(rows)
        for n, i in enumerate(rows):
            for jj in range(7):
                for h in range(2):
                    at = 2 * jj * m + 16 * n + 8 * h
                    e, o = acc[at : at + 8], acc[at + m : at + m + 8]
                    sb[2 * h, i, jj] = jnp.where(sub8 < 4, e, pltpu.roll(o, 4, 0)).astype(BF16)
                    sb[2 * h + 1, i, jj] = jnp.where(sub8 < 4, pltpu.roll(e, 4, 0), o).astype(BF16)

    slot = XB * core + x

    def out_copy(i, k):
        xb = (x + k // 2) % XB
        c = (core + k) % 2
        return pltpu.make_async_remote_copy(
            src_ref=sb.at[xb, i], dst_ref=gb.at[slot, y], send_sem=s_g.at[i, k], recv_sem=r_g.at[slot, y],
            device_id=(xb, z * YB + i, c), device_id_type=MESH,
        )

    def end_out(k, _):
        for i in range(4):

            @pl.when(jnp.logical_not(jnp.logical_and(k == 0, y == i)))
            def _():
                out_copy(i, k).wait_send()

        return 0

    def start_out(i):
        def step(k, _):
            here = jnp.logical_and(k == 0, y == i)

            @pl.when(jnp.logical_not(here))
            def _():
                out_copy(i, k).start()

            return 0

        lax.fori_loop(0, 8, step, 0)

    reduce_rows((1, 2))
    start_out(1)
    start_out(2)
    conv2(0, PAIRS2, ((7, 1),))
    reduce_rows((0,))
    start_out(0)
    send_o.wait()

    def fill_last(i, _):
        v = ho[pl.ds(7 * i, 7)].astype(F32)
        ob[pl.ds(7 * i, 7), 8] = jnp.where(z < ZB - 1, v, 0.0).astype(BF16)
        return 0

    lax.fori_loop(0, 4, fill_last, 0)
    reduce_rows((3,))
    start_out(3)
    own_out = pltpu.make_async_copy(sb.at[x, y], gb.at[slot, y], l_a.at[1])
    own_out.start()
    own_out.wait()

    def wait_out(k, _):
        s, q = k // YB, k % YB

        @pl.when(jnp.logical_not(jnp.logical_and(s == slot, q == y)))
        def _():
            pltpu.make_async_remote_copy(
                src_ref=sb.at[0, 0], dst_ref=gb.at[s, q], send_sem=s_g.at[0, 0], recv_sem=r_g.at[s, q],
                device_id=(x, zy, 1 - core), device_id_type=MESH,
            ).wait_recv()

        return 0

    lax.fori_loop(0, 32, wait_out, 0)

    def select(s, _):
        src = jnp.int32(0)
        length = jnp.int32(0)
        for c in range(8):
            hit = owner[c] == XB * core + s
            src = jnp.where(hit, stored[c], src)
            length = jnp.where(hit, lengths[c], length)
        alive = (XB * x + sub8 % 4) < length
        columns = []
        for q in range(YB):
            tiles = gb[src, q]
            for j in range(JC):
                tile = tiles[j // 2].astype(F32)
                columns.append(tile if j % 2 == 0 else pltpu.roll(tile, 4, 0))
        for g in range(13):
            c0, c1, c2, c3 = columns[4 * g : 4 * g + 4]
            t1, t2, t3 = pltpu.roll(c1, 96, 1), pltpu.roll(c2, 64, 1), pltpu.roll(c3, 32, 1)
            dense = [jnp.where(lane < 96, c0, t1), jnp.where(lane < 64, t1, t2), jnp.where(lane < 32, t2, t3)]
            for m in range(3):
                out[s, :, pl.ds(384 * g + 128 * m, 128)] = jnp.where(alive, dense[m], 0.0)[0:4].astype(BF16)
        return 0

    lax.fori_loop(0, XB, select, 0)

    def end_in(i, _):
        for chunk in range(3):
            in_copy(i, chunk).wait_send()
        return 0

    lax.fori_loop(1, 16, end_in, 0)

    lax.fori_loop(0, 8, end_out, 0)


def local(
    features, lengths, stored_slot, owner_slot, gain_first, conv_first, bias_first,
    gain_second, conv_second, bias_second, reduce_conv_weight, reduce_conv_bias,
):
    slots, frames, rows, lanes = features.shape
    feat = jnp.transpose(features, (0, 2, 1, 3)).reshape(slots, rows * frames, lanes)
    feat = jnp.pad(feat, ((0, 0), (0, 0), (PADL, PADR)))
    hbm = pl.BlockSpec(memory_space=pltpu.HBM)
    dma = pltpu.SemaphoreType.DMA
    result = pl.pallas_call(
        kernel,
        out_shape=jax.ShapeDtypeStruct((slots, frames, 4992), BF16),
        in_specs=[pl.BlockSpec(memory_space=pl.ANY)] + [hbm] * 11,
        out_specs=pl.BlockSpec(memory_space=pltpu.VMEM),
        scratch_shapes=[
            pltpu.VMEM((16, 8, WIN * CH), BF16),
            pltpu.VMEM((WIN, 8, 16, LANES), BF16),
            pltpu.VMEM((3, WIN, 10, 16, LANES), BF16),
            pltpu.VMEM((3, BC, 10, 16, LANES), BF16),
            pltpu.VMEM((9, 512, 256), BF16),
            pltpu.VMEM((9, 512, 256), BF16),
            pltpu.VMEM((1152, 128), BF16),
            pltpu.VMEM((OC, 9, 16, LANES), BF16),
            pltpu.VMEM((XB, 4, 7, 8, LANES), BF16),
            pltpu.VMEM((2 * XB, YB, 7, 8, LANES), BF16),
            pltpu.VMEM((2, WIN, 16, LANES), BF16),
            pltpu.VMEM((2, BC, 16, LANES), BF16),
            pltpu.VMEM((OC, 16, LANES), BF16),
            pltpu.VMEM((27, CH, CH), BF16),
            pltpu.VMEM((27, CH, CH), BF16),
            pltpu.VMEM((9, CH, CH), BF16),
            pltpu.VMEM((5, 1, CH), F32),
            pltpu.VMEM((8, LANES), F32),
            pltpu.VMEM((256, 256), BF16),
            pltpu.SMEM((8,), jnp.int32),
            pltpu.SMEM((8,), jnp.int32),
            pltpu.SMEM((8,), jnp.int32),
            dma((3, 16)),
            dma((3, 16)),
            dma((13,)),
            dma((13,)),
            dma((4, 8)),
            dma((8, 4)),
            dma((2,)),
            dma((11,)),
        ],
        compiler_params=pltpu.CompilerParams(
            collective_id=0, has_side_effects=True, vmem_limit_bytes=60 << 20
        ),
        name="encode",
    )(
        feat,
        conv_first.reshape(27, CH, CH),
        conv_second.reshape(27, CH, CH),
        reduce_conv_weight.reshape(9, CH, CH),
        *[v.reshape(1, CH) for v in (gain_first, bias_first, gain_second, bias_second, reduce_conv_bias)],
        lengths, stored_slot, owner_slot,
    )
    return result.reshape(slots, frames, 1, 4992)


def solution(mesh):
    spec = P("clip", "tm", "rows", None)
    return jax.shard_map(
        local, mesh=mesh, in_specs=(spec,) + (P(),) * 11, out_specs=spec, check_vma=False
    )
```

```python
import jax
import jax.numpy as jnp
from jax import lax
from jax.experimental import pallas as pl
from jax.experimental.pallas import tpu as pltpu
from jax.sharding import PartitionSpec as P

NORM_EPS = 1e-06
MESH = pl.DeviceIdType.MESH
F32 = jnp.float32
BF16 = jnp.bfloat16

CH = 96
XB = 4
YB = 4
ZB = 8
OWN = 26
GROUPS = 9
WIN = GROUPS * 4
PADL = 384
PADR = 768
LANES = 128
PAIRS1 = 15
PAIRS2 = 14
BC = 2 * PAIRS1
OC = 2 * PAIRS2
JC = 13


def shifted(flat, step, frame):
    return jnp.where(frame < step, 0.0, pltpu.roll(flat, step, 0))


def split_square(v):
    sq = v * v
    hi = sq.astype(BF16)
    return hi, (sq - hi.astype(F32)).astype(BF16)


def scaled_act(v, total, half_gain):
    half = v * lax.rsqrt(total * (1.0 / CH) + NORM_EPS) * half_gain
    return half + half * jnp.tanh(half)


def build_toeplitz(w_ref, wt):
    def tap(i, _):
        for n in range(2):
            for k in range(3):
                wt[i, pl.ds(128 * (n + k), CH), pl.ds(128 * n, CH)] = w_ref[3 * i + k]
        return 0

    lax.fori_loop(0, 9, tap, 0)


def conv_lhs(src, col0, pairs, rows):
    parts = []
    for t in range(3):
        for j in range(3):
            for k in range(4):
                pieces = []
                for p in range(pairs):
                    for first, count in rows:
                        block = src[t, col0 + 2 * p + k, first + j : first + j + count]
                        pieces.append(block.reshape(count * 16, LANES))
                parts.append(jnp.concatenate(pieces, axis=0))
    return jnp.concatenate(parts, axis=1)


INNER = ((1, 6),)
EDGES = ((0, 1), (7, 1))
EDGES2 = ((0, 1), (7, 2))


def kernel(
    feat, w1h, w2h, wrh, g1h, b1h, g2h, b2h, brh, lenh, stoh, ownh, out,
    arr, xs, a, b, wt1, wt2, rw, ob, sb, gb, ha, hb, w1, w2, wr, vin, vec, ones2,
    lengths, stored, owner,
    s_a, r_a, s_z, r_z, s_g, r_g, l_a, l_w,
):
    x = lax.axis_index("tm")
    zy = lax.axis_index("rows")
    core = lax.axis_index("clip")
    z, y = zy // YB, zy % YB
    me = x * YB + y
    up = ((z + ZB - 1) % ZB) * YB + y
    down = ((z + 1) % ZB) * YB + y

    def plane(i):
        t = (me + i) % 16
        return t, (t // YB, z * YB + t % YB, core)

    def start_lane(q):
        return pl.multiple_of(PADL + CH * (OWN * q - 4 + 2 * (q % 2)), 128)

    arr[:, :, 0:128] = jnp.zeros((16, 8, 128), BF16)
    arr[:, :, 3072:3456] = jnp.zeros((16, 8, 384), BF16)
    barrier = pltpu.get_barrier_semaphore()

    xs_of = [(x + d) % XB for d in range(XB)]
    ys_of = [(y + d) % YB for d in range(YB)]
    for dx in range(XB):
        for dy in range(YB):
            if dx or dy:
                dev = (xs_of[dx], z * YB + ys_of[dy], core)
                pl.semaphore_signal(barrier, inc=1, device_id=dev, device_id_type=MESH)
    for dev in ((x, up, core), (x, down, core), (x, zy, 1 - core)):
        pl.semaphore_signal(barrier, inc=1, device_id=dev, device_id_type=MESH)

    loads = [
        pltpu.make_async_copy(src, dst, l_w.at[i])
        for i, (src, dst) in enumerate(
            [(w1h, w1), (w2h, w2), (wrh, wr)]
            + [(v, vin.at[i]) for i, v in enumerate((g1h, b1h, g2h, b2h, brh))]
            + [(lenh, lengths), (stoh, stored), (ownh, owner)]
        )
    ]
    for c in loads:
        c.start()

    def zero_weights(i, _):
        wt1[i] = jnp.zeros((512, 256), BF16)
        wt2[i] = jnp.zeros((512, 256), BF16)
        return 0

    lax.fori_loop(0, 9, zero_weights, 0)
    rw[...] = jnp.zeros_like(rw)
    vec[...] = jnp.zeros_like(vec)
    r_i = lax.broadcasted_iota(jnp.int32, (256, 256), 0) // 128
    c_i = lax.broadcasted_iota(jnp.int32, (256, 256), 1) // 128
    ones2[...] = jnp.where(r_i == c_i, 1.0, 0.0).astype(BF16)
    loads[0].wait()
    build_toeplitz(w1, wt1)
    pl.semaphore_wait(barrier, 18)

    HALF = 1024
    odd = y % 2

    def in_copy(i, chunk):
        t, dev = plane(i)
        q = t % YB
        off = 128 * (1 - q % 2) + HALF * chunk
        src = feat.at[t // YB, :, pl.ds(pl.multiple_of(start_lane(q) + off, 128), HALF)]
        dst = arr.at[me, :, pl.ds(pl.multiple_of(off, 128), HALF)]
        return pltpu.make_async_remote_copy(
            src_ref=src, dst_ref=dst, send_sem=s_a.at[chunk, t], recv_sem=r_a.at[chunk, me],
            device_id=dev, device_id_type=MESH,
        )

    my_off = 128 * (1 - odd)
    own_in = pltpu.make_async_copy(
        feat.at[x, :, pl.ds(pl.multiple_of(start_lane(y) + my_off, 128), 3 * HALF)],
        arr.at[me, :, pl.ds(pl.multiple_of(my_off, 128), 3 * HALF)],
        l_a.at[0],
    )
    own_in.start()

    def start_in(i, _):
        in_copy(i % 15 + 1, i // 15).start()
        return 0

    lax.fori_loop(0, 45, start_in, 0)

    for c in loads[1:]:
        c.wait()
    build_toeplitz(w2, wt2)

    def tap(i, _):
        rw[pl.ds(pl.multiple_of(128 * i, 128), CH), pl.ds(0, CH)] = wr[i]
        return 0

    lax.fori_loop(0, 9, tap, 0)
    for i in range(5):
        vec[i : i + 1, 0:CH] = vin[i]
    gain1, bias1, gain2, bias2, bias_r = [vec[i : i + 1] for i in range(5)]
    gain1, gain2 = 0.5 * gain1, 0.5 * gain2
    bias1w = jnp.concatenate([bias1, bias1], axis=1)
    gain2w = jnp.concatenate([gain2, gain2], axis=1)
    bias2w = jnp.concatenate([bias2, bias2], axis=1)

    own_in.wait()

    def wait_in(chunk):
        def step(i, _):
            t, dev = plane(i)
            dst = arr.at[t, :, pl.ds(pl.multiple_of(my_off + HALF * chunk, 128), HALF)]
            pltpu.make_async_remote_copy(
                src_ref=feat.at[0, :, pl.ds(0, HALF)], dst_ref=dst,
                send_sem=s_a.at[chunk, t], recv_sem=r_a.at[chunk, t],
                device_id=dev, device_id_type=MESH,
            ).wait_recv()
            return 0

        lax.fori_loop(1, 16, step, 0)

    lane = lax.broadcasted_iota(jnp.int32, (8, LANES), 1)
    sub8 = lax.broadcasted_iota(jnp.int32, (8, LANES), 0)
    ones1 = jnp.ones((256, LANES), BF16)
    frame128 = lax.broadcasted_iota(jnp.int32, (128, LANES), 0) % 16

    def act_group(q, g):
        lane0 = pl.multiple_of(g * 384, 128)
        cols = [[] for _ in range(4)]
        for xb in range(XB):
            v = [arr[XB * xb + q, :, pl.ds(lane0 + 128 * m, 128)].astype(F32) for m in range(3)]
            cols[0].append(jnp.where(lane < 96, v[0], 0.0))
            cols[1].append(
                jnp.where(lane < 32, pltpu.roll(v[0], 32, 1), jnp.where(lane < 96, pltpu.roll(v[1], 32, 1), 0.0))
            )
            cols[2].append(
                jnp.where(lane < 64, pltpu.roll(v[1], 64, 1), jnp.where(lane < 96, pltpu.roll(v[2], 64, 1), 0.0))
            )
            cols[3].append(jnp.where(lane < 96, pltpu.roll(v[2], 96, 1), 0.0))
        tiles = []
        for c in cols:
            turned = [pltpu.roll(u, 4, 0) for u in c]
            tiles += [jnp.where(sub8 < 4, c[0], turned[1]), jnp.where(sub8 < 4, c[2], turned[3])]
            tiles += [jnp.where(sub8 < 4, turned[0], c[1]), jnp.where(sub8 < 4, turned[2], c[3])]
        return jnp.concatenate(tiles, axis=0)

    def act_store(flat, total, q, g):
        w0 = 4 * g
        row = 2 * q
        xs[pl.ds(w0, 4), pl.ds(row, 2)] = flat.astype(BF16).reshape(4, 2, 16, LANES)
        act = scaled_act(flat, total, gain1)
        for t in range(3):
            moved = act if t == 2 else shifted(act, 2 - t, frame128)
            a[t, pl.ds(w0, 4), pl.ds(row + 1, 2)] = moved.astype(BF16).reshape(4, 2, 16, LANES)

    def act_step(i, qs):
        flats = [act_group(q, i) for q in qs]
        hi, lo = split_square(jnp.concatenate(flats, axis=0))
        total = jnp.dot(jnp.concatenate([hi, lo], axis=1), ones1, preferred_element_type=F32)
        for m, q in enumerate(qs):
            act_store(flats[m], total[128 * m : 128 * m + 128], q, i)
        return 0

    def z_copy(src, dst, k, row):
        return pltpu.make_async_remote_copy(
            src_ref=src, dst_ref=dst, send_sem=s_z.at[k], recv_sem=r_z.at[k],
            device_id=(x, row, core), device_id_type=MESH,
        )

    inside = (z > 0, z < ZB - 1)

    def fill_halo(halo, dst, count, unit, sides):
        frame = lax.broadcasted_iota(jnp.int32, (16 * unit, LANES), 0) % 16

        def step(i, _):
            c = unit * i
            for side, row in enumerate(sides):
                v = halo[side, pl.ds(c, unit)].astype(F32).reshape(16 * unit, LANES)
                v = jnp.where(inside[min(side, 1)], v, 0.0)
                for t in range(3):
                    moved = v if t == 2 else shifted(v, 2 - t, frame)
                    dst[t, pl.ds(c, unit), row] = moved.astype(BF16).reshape(unit, 16, LANES)
            return 0

        lax.fori_loop(0, count // unit, step, 0)

    base = 2 * (1 - odd)
    col0 = OWN * y

    def conv1(p0, pairs, rows):
        acc = jnp.dot(
            conv_lhs(a, base + 2 * p0, pairs, rows), wt1[...].reshape(4608, 256), preferred_element_type=F32
        )
        v = acc + bias1w
        hi, lo = split_square(v)
        total = jnp.dot(hi, ones2[...], preferred_element_type=F32) + jnp.dot(
            lo, ones2[...], preferred_element_type=F32
        )
        act = scaled_act(v, total, gain2w)
        height = sum(count for _, count in rows)
        m = 16 * height
        frame = lax.broadcasted_iota(jnp.int32, (m, LANES), 0) % 16
        for p in range(pairs):
            for n in range(2):
                bcol = 2 * (p0 + p) + n
                image = col0 - 1 + bcol
                u = act[m * p : m * p + m, 128 * n : 128 * n + 128]
                u = jnp.where(jnp.logical_and(image >= 0, image < 104), u, 0.0)
                for t in range(3):
                    moved = (u if t == 2 else shifted(u, 2 - t, frame)).astype(BF16)
                    at = 0
                    for first, count in rows:
                        b[t, bcol, first + 1 : first + 1 + count] = moved[16 * at : 16 * (at + count)].reshape(
                            count, 16, LANES
                        )
                        at += count

    def conv2(p0, pairs, rows):
        acc = jnp.dot(
            conv_lhs(b, 2 * p0, pairs, rows), wt2[...].reshape(4608, 256), preferred_element_type=F32
        )
        v = acc + bias2w
        height = sum(count for _, count in rows)
        m = 16 * height
        for p in range(pairs):
            for n in range(2):
                c = 2 * (p0 + p) + n
                u = v[m * p : m * p + m, 128 * n : 128 * n + 128]
                at = 0
                for first, count in rows:
                    part = u[16 * at : 16 * (at + count)]
                    part = part + xs[base + 2 + c, first : first + count].reshape(16 * count, LANES).astype(F32)
                    part = jnp.where(col0 + c < 104, part, 0.0).astype(BF16).reshape(count, 16, LANES)
                    if first + count == 9:
                        ob[c, first : first + count - 1] = part[: count - 1]
                        ob[c, 8:9] = jnp.where(z < ZB - 1, part[count - 1 :], 0.0).astype(BF16)
                    else:
                        ob[c, first : first + count] = part
                    at += count

    def inner1(i, _):
        conv1(3 * i, 3, INNER)
        return 0

    def a_copies(g):
        part = pl.ds(4 * g, 4)
        return (
            z_copy(a.at[2, part, 1], ha.at[1, part], g, up),
            z_copy(a.at[2, part, 8], ha.at[0, part], 9 + g, down),
            z_copy(xs.at[part, 0], xs.at[part, 8], 18 + g, up),
        )

    def outer_rows(g, _):
        act_step(g, (0, 3))
        for c in a_copies(g):
            c.start()
        return 0

    def inner_rows(g, _):
        return act_step(g, (1, 2))

    def chunk_step(chunk, _):
        wait_in(chunk)
        g0, g1 = chunk * (chunk + 3) // 2, (chunk + 1) * (chunk + 4) // 2
        lax.fori_loop(g0, g1, outer_rows, 0)
        lax.fori_loop(g0, g1, inner_rows, 0)
        p0 = jnp.maximum(chunk - 1, 0)
        lax.fori_loop(p0 * (p0 + 3) // 2, chunk * (chunk + 3) // 2, inner1, 0)
        return 0

    lax.fori_loop(0, 3, chunk_step, 0)
    early_b = z_copy(b.at[2, :, 2], hb.at[2], 33, up)
    early_b.start()

    def end_a(g, _):
        for c in a_copies(g):
            c.wait()
        return 0

    lax.fori_loop(0, GROUPS, end_a, 0)
    fill_halo(ha, a, WIN, 4, (0, 9))

    def b_copies(e):
        part = pl.ds(10 * e, 10)
        return (
            z_copy(b.at[2, part, 1], hb.at[1, part], 27 + e, up),
            z_copy(b.at[2, part, 8], hb.at[0, part], 30 + e, down),
        )

    def edge1(e, _):
        conv1(5 * e, 5, EDGES)
        for c in b_copies(e):
            c.start()
        return 0

    lax.fori_loop(0, 3, edge1, 0)

    def inner2(i, _):
        conv2(7 * i, 7, INNER)
        return 0

    lax.fori_loop(0, 2, inner2, 0)

    def reduce_rows(rows):
        pieces = []
        for j2 in range(3):
            for k in range(3):
                tiles = []
                for j in range(14):
                    c = min(2 * j + k, OC - 1)
                    tiles += [ob[c, 2 * i + j2] for i in rows]
                pieces.append(jnp.concatenate(tiles, axis=0))
        acc = jnp.dot(jnp.concatenate(pieces, axis=1), rw[...], preferred_element_type=F32) + bias_r
        m = 16 * len(rows)
        for n, i in enumerate(rows):
            for jj in range(7):
                for h in range(2):
                    at = 2 * jj * m + 16 * n + 8 * h
                    e, o = acc[at : at + 8], acc[at + m : at + m + 8]
                    sb[2 * h, i, jj] = jnp.where(sub8 < 4, e, pltpu.roll(o, 4, 0)).astype(BF16)
                    sb[2 * h + 1, i, jj] = jnp.where(sub8 < 4, pltpu.roll(e, 4, 0), o).astype(BF16)

    slot = XB * core + x

    def out_copy(i, k):
        xb = (x + k // 2) % XB
        c = (core + k) % 2
        return pltpu.make_async_remote_copy(
            src_ref=sb.at[xb, i], dst_ref=gb.at[slot, y], send_sem=s_g.at[i, k], recv_sem=r_g.at[slot, y],
            device_id=(xb, z * YB + i, c), device_id_type=MESH,
        )

    def end_out(k, _):
        for i in range(4):

            @pl.when(jnp.logical_not(jnp.logical_and(k == 0, y == i)))
            def _():
                out_copy(i, k).wait_send()

        return 0

    def start_out(i):
        def step(k, _):
            here = jnp.logical_and(k == 0, y == i)

            @pl.when(jnp.logical_not(here))
            def _():
                out_copy(i, k).start()

            return 0

        lax.fori_loop(0, 8, step, 0)

    reduce_rows((1, 2))
    start_out(1)
    start_out(2)
    early_b.wait()

    def end_b(e, _):
        for c in b_copies(e):
            c.wait()
        return 0

    lax.fori_loop(0, 3, end_b, 0)
    fill_halo(hb, b, BC, 5, (0, 9, 10))

    def edge2(i, _):
        conv2(7 * i, 7, EDGES2)
        return 0

    lax.fori_loop(0, 2, edge2, 0)
    reduce_rows((0, 3))
    start_out(0)
    start_out(3)
    own_out = pltpu.make_async_copy(sb.at[x, y], gb.at[slot, y], l_a.at[1])
    own_out.start()
    own_out.wait()

    def wait_out(k, _):
        s, q = k // YB, k % YB

        @pl.when(jnp.logical_not(jnp.logical_and(s == slot, q == y)))
        def _():
            pltpu.make_async_remote_copy(
                src_ref=sb.at[0, 0], dst_ref=gb.at[s, q], send_sem=s_g.at[0, 0], recv_sem=r_g.at[s, q],
                device_id=(x, zy, 1 - core), device_id_type=MESH,
            ).wait_recv()

        return 0

    lax.fori_loop(0, 32, wait_out, 0)

    def select(s, _):
        src = jnp.int32(0)
        length = jnp.int32(0)
        for c in range(8):
            hit = owner[c] == XB * core + s
            src = jnp.where(hit, stored[c], src)
            length = jnp.where(hit, lengths[c], length)
        alive = (XB * x + sub8 % 4) < length
        columns = []
        for q in range(YB):
            tiles = gb[src, q]
            for j in range(JC):
                tile = tiles[j // 2].astype(F32)
                columns.append(tile if j % 2 == 0 else pltpu.roll(tile, 4, 0))
        for g in range(13):
            c0, c1, c2, c3 = columns[4 * g : 4 * g + 4]
            t1, t2, t3 = pltpu.roll(c1, 96, 1), pltpu.roll(c2, 64, 1), pltpu.roll(c3, 32, 1)
            dense = [jnp.where(lane < 96, c0, t1), jnp.where(lane < 64, t1, t2), jnp.where(lane < 32, t2, t3)]
            for m in range(3):
                out[s, :, pl.ds(384 * g + 128 * m, 128)] = jnp.where(alive, dense[m], 0.0)[0:4].astype(BF16)
        return 0

    lax.fori_loop(0, XB, select, 0)

    def end_in(i, _):
        for chunk in range(3):
            in_copy(i, chunk).wait_send()
        return 0

    lax.fori_loop(1, 16, end_in, 0)

    lax.fori_loop(0, 8, end_out, 0)


def local(
    features, lengths, stored_slot, owner_slot, gain_first, conv_first, bias_first,
    gain_second, conv_second, bias_second, reduce_conv_weight, reduce_conv_bias,
):
    slots, frames, rows, lanes = features.shape
    feat = jnp.transpose(features, (0, 2, 1, 3)).reshape(slots, rows * frames, lanes)
    feat = jnp.pad(feat, ((0, 0), (0, 0), (PADL, PADR)))
    hbm = pl.BlockSpec(memory_space=pltpu.HBM)
    dma = pltpu.SemaphoreType.DMA
    result = pl.pallas_call(
        kernel,
        out_shape=jax.ShapeDtypeStruct((slots, frames, 4992), BF16),
        in_specs=[pl.BlockSpec(memory_space=pl.ANY)] + [hbm] * 11,
        out_specs=pl.BlockSpec(memory_space=pltpu.VMEM),
        scratch_shapes=[
            pltpu.VMEM((16, 8, WIN * CH), BF16),
            pltpu.VMEM((WIN, 9, 16, LANES), BF16),
            pltpu.VMEM((3, WIN, 10, 16, LANES), BF16),
            pltpu.VMEM((3, BC, 11, 16, LANES), BF16),
            pltpu.VMEM((9, 512, 256), BF16),
            pltpu.VMEM((9, 512, 256), BF16),
            pltpu.VMEM((1152, 128), BF16),
            pltpu.VMEM((OC, 9, 16, LANES), BF16),
            pltpu.VMEM((XB, 4, 7, 8, LANES), BF16),
            pltpu.VMEM((2 * XB, YB, 7, 8, LANES), BF16),
            pltpu.VMEM((2, WIN, 16, LANES), BF16),
            pltpu.VMEM((3, BC, 16, LANES), BF16),
            pltpu.VMEM((27, CH, CH), BF16),
            pltpu.VMEM((27, CH, CH), BF16),
            pltpu.VMEM((9, CH, CH), BF16),
            pltpu.VMEM((5, 1, CH), F32),
            pltpu.VMEM((8, LANES), F32),
            pltpu.VMEM((256, 256), BF16),
            pltpu.SMEM((8,), jnp.int32),
            pltpu.SMEM((8,), jnp.int32),
            pltpu.SMEM((8,), jnp.int32),
            dma((3, 16)),
            dma((3, 16)),
            dma((34,)),
            dma((34,)),
            dma((4, 8)),
            dma((8, 4)),
            dma((2,)),
            dma((11,)),
        ],
        compiler_params=pltpu.CompilerParams(
            collective_id=0, has_side_effects=True, vmem_limit_bytes=50 << 20
        ),
        name="encode",
    )(
        feat,
        conv_first.reshape(27, CH, CH),
        conv_second.reshape(27, CH, CH),
        reduce_conv_weight.reshape(9, CH, CH),
        *[v.reshape(1, CH) for v in (gain_first, bias_first, gain_second, bias_second, reduce_conv_bias)],
        lengths, stored_slot, owner_slot,
    )
    return result.reshape(slots, frames, 1, 4992)


def solution(mesh):
    spec = P("clip", "tm", "rows", None)
    return jax.shard_map(
        local, mesh=mesh, in_specs=(spec,) + (P(),) * 11, out_specs=spec, check_vma=False
    )
```

```python
import jax
import jax.numpy as jnp
from jax import lax
from jax.experimental import pallas as pl
from jax.experimental.pallas import tpu as pltpu
from jax.sharding import PartitionSpec as P

NORM_EPS = 1e-06
MESH = pl.DeviceIdType.MESH
F32 = jnp.float32
BF16 = jnp.bfloat16

CH = 96
XB = 4
YB = 4
ZB = 8
OWN = 26
GROUPS = 9
WIN = GROUPS * 4
LANES = 128
PAIRS1 = 15
PAIRS2 = 14
BC = 2 * PAIRS1
OC = 2 * PAIRS2
JC = 13


def shifted(flat, step, frame):
    return jnp.where(frame < step, 0.0, pltpu.roll(flat, step, 0))


def split_square(v):
    sq = v * v
    hi = sq.astype(BF16)
    return hi, (sq - hi.astype(F32)).astype(BF16)


def scaled_act(v, total, half_gain):
    half = v * lax.rsqrt(total * (1.0 / CH) + NORM_EPS) * half_gain
    return half + half * jnp.tanh(half)


def build_toeplitz(w_ref, wt):
    def tap(i, _):
        for n in range(2):
            for k in range(3):
                wt[i, pl.ds(128 * (n + k), CH), pl.ds(128 * n, CH)] = w_ref[3 * i + k]
        return 0

    lax.fori_loop(0, 9, tap, 0)


def conv_lhs(src, col0, pairs, rows):
    parts = []
    for t in range(3):
        for j in range(3):
            for k in range(4):
                pieces = []
                for p in range(pairs):
                    for first, count in rows:
                        block = src[t, col0 + 2 * p + k, first + j : first + j + count]
                        pieces.append(block.reshape(count * 16, LANES))
                parts.append(jnp.concatenate(pieces, axis=0))
    return jnp.concatenate(parts, axis=1)


INNER = ((1, 6),)
AROUND = sorted(
    ((dx, dy) for dx in range(4) for dy in range(4) if dx or dy),
    key=lambda d: -(min(d[0], 4 - d[0]) + min(d[1], 4 - d[1])),
)
EDGES = ((0, 1), (7, 1))
EDGES2 = ((0, 1), (7, 2))


def kernel(
    feat, w1h, w2h, wrh, g1h, b1h, g2h, b2h, brh, lenh, stoh, ownh, out,
    arr, xs, a, b, wt1, wt2, rw, ob, sb, gb, ha, hb, w1, w2, wr, vin, vec, ones2,
    lengths, stored, owner,
    s_a, r_a, s_z, r_z, s_g, r_g, l_a, l_w,
):
    x = lax.axis_index("tm")
    zy = lax.axis_index("rows")
    core = lax.axis_index("clip")
    z, y = zy // YB, zy % YB
    me = x * YB + y
    up = ((z + ZB - 1) % ZB) * YB + y
    down = ((z + 1) % ZB) * YB + y

    def plane(i):
        t = (me + i) % 16
        return t, (t // YB, z * YB + t % YB, core)

    def start_lane(q):
        return 2304 * q + 128 * (q // 2 - q // 3)

    def place(q):
        return 384 * (1 - (q + 3) // 4) + 128 * (q // 2 - q // 3)

    arr[:, :, 0:384] = jnp.zeros((16, 8, 384), BF16)
    arr[:, :, 3072:3456] = jnp.zeros((16, 8, 384), BF16)
    barrier = pltpu.get_barrier_semaphore()

    xs_of = [(x + d) % XB for d in range(XB)]
    ys_of = [(y + d) % YB for d in range(YB)]
    for dx in range(XB):
        for dy in range(YB):
            if dx or dy:
                dev = (xs_of[dx], z * YB + ys_of[dy], core)
                pl.semaphore_signal(barrier, inc=1, device_id=dev, device_id_type=MESH)
    for dev in ((x, up, core), (x, down, core), (x, zy, 1 - core)):
        pl.semaphore_signal(barrier, inc=1, device_id=dev, device_id_type=MESH)

    loads = [
        pltpu.make_async_copy(src, dst, l_w.at[i])
        for i, (src, dst) in enumerate(
            [(w1h, w1), (w2h, w2), (wrh, wr)]
            + [(v, vin.at[i]) for i, v in enumerate((g1h, b1h, g2h, b2h, brh))]
            + [(lenh, lengths), (stoh, stored), (ownh, owner)]
        )
    ]
    for c in loads:
        c.start()

    def zero_weights(i, _):
        wt1[i] = jnp.zeros((512, 256), BF16)
        wt2[i] = jnp.zeros((512, 256), BF16)
        return 0

    lax.fori_loop(0, 9, zero_weights, 0)
    rw[...] = jnp.zeros_like(rw)
    vec[...] = jnp.zeros_like(vec)
    r_i = lax.broadcasted_iota(jnp.int32, (256, 256), 0) // 128
    c_i = lax.broadcasted_iota(jnp.int32, (256, 256), 1) // 128
    ones2[...] = jnp.where(r_i == c_i, 1.0, 0.0).astype(BF16)
    loads[0].wait()
    build_toeplitz(w1, wt1)
    pl.semaphore_wait(barrier, 18)

    HALF = 1024

    starts = [start_lane(v) for v in ys_of]
    offs = [place(v) for v in ys_of]

    def in_copy(dx, dy, chunk):
        src = feat.at[xs_of[dx], :, pl.ds(pl.multiple_of(starts[dy] + HALF * chunk, 128), HALF)]
        dst = arr.at[me, :, pl.ds(pl.multiple_of(offs[dy] + HALF * chunk, 128), HALF)]
        return pltpu.make_async_remote_copy(
            src_ref=src, dst_ref=dst,
            send_sem=s_a.at[chunk, 4 * dx + dy],
            recv_sem=r_a.at[chunk, 4 * ((4 - dx) % 4) + (4 - dy) % 4],
            device_id=(xs_of[dx], z * YB + ys_of[dy], core), device_id_type=MESH,
        )

    my_off = place(y)
    own_in = pltpu.make_async_copy(
        feat.at[x, :, pl.ds(pl.multiple_of(start_lane(y), 128), 3 * HALF)],
        arr.at[me, :, pl.ds(pl.multiple_of(my_off, 128), 3 * HALF)],
        l_a.at[0],
    )
    own_in.start()

    def start_in(chunk, _):
        for dx, dy in AROUND:
            in_copy(dx, dy, chunk).start()
        return 0

    lax.fori_loop(0, 3, start_in, 0)

    for c in loads[1:]:
        c.wait()
    build_toeplitz(w2, wt2)

    def tap(i, _):
        rw[pl.ds(pl.multiple_of(128 * i, 128), CH), pl.ds(0, CH)] = wr[i]
        return 0

    lax.fori_loop(0, 9, tap, 0)
    for i in range(5):
        vec[i : i + 1, 0:CH] = vin[i]
    gain1, bias1, gain2, bias2, bias_r = [vec[i : i + 1] for i in range(5)]
    gain1, gain2 = 0.5 * gain1, 0.5 * gain2
    bias1w = jnp.concatenate([bias1, bias1], axis=1)
    gain2w = jnp.concatenate([gain2, gain2], axis=1)
    bias2w = jnp.concatenate([bias2, bias2], axis=1)

    own_in.wait()

    def wait_in(chunk):
        for dx, dy in AROUND:
            t = YB * xs_of[dx] + ys_of[dy]
            dst = arr.at[t, :, pl.ds(pl.multiple_of(my_off + HALF * chunk, 128), HALF)]
            pltpu.make_async_remote_copy(
                src_ref=feat.at[0, :, pl.ds(0, HALF)], dst_ref=dst,
                send_sem=s_a.at[chunk, 4 * dx + dy], recv_sem=r_a.at[chunk, 4 * dx + dy],
                device_id=(xs_of[dx], z * YB + ys_of[dy], core), device_id_type=MESH,
            ).wait_recv()

    lane = lax.broadcasted_iota(jnp.int32, (8, LANES), 1)
    sub8 = lax.broadcasted_iota(jnp.int32, (8, LANES), 0)
    ones1 = jnp.ones((256, LANES), BF16)
    frame128 = lax.broadcasted_iota(jnp.int32, (128, LANES), 0) % 16

    def act_group(q, g):
        lane0 = pl.multiple_of(g * 384, 128)
        cols = [[] for _ in range(4)]
        for xb in range(XB):
            v = [arr[XB * xb + q, :, pl.ds(lane0 + 128 * m, 128)].astype(F32) for m in range(3)]
            cols[0].append(jnp.where(lane < 96, v[0], 0.0))
            cols[1].append(
                jnp.where(lane < 32, pltpu.roll(v[0], 32, 1), jnp.where(lane < 96, pltpu.roll(v[1], 32, 1), 0.0))
            )
            cols[2].append(
                jnp.where(lane < 64, pltpu.roll(v[1], 64, 1), jnp.where(lane < 96, pltpu.roll(v[2], 64, 1), 0.0))
            )
            cols[3].append(jnp.where(lane < 96, pltpu.roll(v[2], 96, 1), 0.0))
        tiles = []
        for c in cols:
            turned = [pltpu.roll(u, 4, 0) for u in c]
            tiles += [jnp.where(sub8 < 4, c[0], turned[1]), jnp.where(sub8 < 4, c[2], turned[3])]
            tiles += [jnp.where(sub8 < 4, turned[0], c[1]), jnp.where(sub8 < 4, turned[2], c[3])]
        return jnp.concatenate(tiles, axis=0)

    def act_store(flat, total, q, g):
        w0 = 4 * g
        row = 2 * q
        xs[pl.ds(w0, 4), pl.ds(row, 2)] = flat.astype(BF16).reshape(4, 2, 16, LANES)
        act = scaled_act(flat, total, gain1)
        for t in range(3):
            moved = act if t == 2 else shifted(act, 2 - t, frame128)
            a[t, pl.ds(w0, 4), pl.ds(row + 1, 2)] = moved.astype(BF16).reshape(4, 2, 16, LANES)

    def act_step(i, qs):
        flats = [act_group(q, i) for q in qs]
        hi, lo = split_square(jnp.concatenate(flats, axis=0))
        total = jnp.dot(jnp.concatenate([hi, lo], axis=1), ones1, preferred_element_type=F32)
        for m, q in enumerate(qs):
            act_store(flats[m], total[128 * m : 128 * m + 128], q, i)
        return 0

    def z_copy(src, dst, k, row):
        return pltpu.make_async_remote_copy(
            src_ref=src, dst_ref=dst, send_sem=s_z.at[k], recv_sem=r_z.at[k],
            device_id=(x, row, core), device_id_type=MESH,
        )

    inside = (z > 0, z < ZB - 1)

    def fill_halo(halo, dst, count, unit, sides):
        frame = lax.broadcasted_iota(jnp.int32, (16 * unit, LANES), 0) % 16

        def step(i, _):
            c = unit * i
            for side, row in enumerate(sides):
                v = halo[side, pl.ds(c, unit)].astype(F32).reshape(16 * unit, LANES)
                v = jnp.where(inside[min(side, 1)], v, 0.0)
                for t in range(3):
                    moved = v if t == 2 else shifted(v, 2 - t, frame)
                    dst[t, pl.ds(c, unit), row] = moved.astype(BF16).reshape(unit, 16, LANES)
            return 0

        lax.fori_loop(0, count // unit, step, 0)

    base = 2 * (1 - y % 2) + 4 * (y // 3)
    col0 = OWN * y

    def conv1(p0, pairs, rows):
        acc = jnp.dot(
            conv_lhs(a, base + 2 * p0, pairs, rows), wt1[...].reshape(4608, 256), preferred_element_type=F32
        )
        v = acc + bias1w
        hi, lo = split_square(v)
        total = jnp.dot(hi, ones2[...], preferred_element_type=F32) + jnp.dot(
            lo, ones2[...], preferred_element_type=F32
        )
        act = scaled_act(v, total, gain2w)
        height = sum(count for _, count in rows)
        m = 16 * height
        frame = lax.broadcasted_iota(jnp.int32, (m, LANES), 0) % 16
        for p in range(pairs):
            for n in range(2):
                bcol = 2 * (p0 + p) + n
                image = col0 - 1 + bcol
                u = act[m * p : m * p + m, 128 * n : 128 * n + 128]
                u = jnp.where(jnp.logical_and(image >= 0, image < 104), u, 0.0)
                for t in range(3):
                    moved = (u if t == 2 else shifted(u, 2 - t, frame)).astype(BF16)
                    at = 0
                    for first, count in rows:
                        b[t, bcol, first + 1 : first + 1 + count] = moved[16 * at : 16 * (at + count)].reshape(
                            count, 16, LANES
                        )
                        at += count

    def conv2(p0, pairs, rows):
        acc = jnp.dot(
            conv_lhs(b, 2 * p0, pairs, rows), wt2[...].reshape(4608, 256), preferred_element_type=F32
        )
        v = acc + bias2w
        height = sum(count for _, count in rows)
        m = 16 * height
        for p in range(pairs):
            for n in range(2):
                c = 2 * (p0 + p) + n
                u = v[m * p : m * p + m, 128 * n : 128 * n + 128]
                at = 0
                for first, count in rows:
                    part = u[16 * at : 16 * (at + count)]
                    part = part + xs[base + 2 + c, first : first + count].reshape(16 * count, LANES).astype(F32)
                    part = jnp.where(col0 + c < 104, part, 0.0).astype(BF16).reshape(count, 16, LANES)
                    if first + count == 9:
                        ob[c, first : first + count - 1] = part[: count - 1]
                        ob[c, 8:9] = jnp.where(z < ZB - 1, part[count - 1 :], 0.0).astype(BF16)
                    else:
                        ob[c, first : first + count] = part
                    at += count

    def inner1(i, _):
        conv1(3 * i, 3, INNER)
        return 0

    def a_copies(g):
        part = pl.ds(4 * g, 4)
        return (
            z_copy(a.at[2, part, 1], ha.at[1, part], g, up),
            z_copy(a.at[2, part, 8], ha.at[0, part], 9 + g, down),
            z_copy(xs.at[part, 0], xs.at[part, 8], 18 + g, up),
        )

    def outer_rows(g, _):
        act_step(g, (0, 3))
        for c in a_copies(g):
            c.start()
        return 0

    def inner_rows(g, _):
        return act_step(g, (1, 2))

    def chunk_step(chunk, _):
        wait_in(chunk)
        g0, g1 = chunk * (chunk + 3) // 2, (chunk + 1) * (chunk + 4) // 2
        lax.fori_loop(g0, g1, outer_rows, 0)
        lax.fori_loop(g0, g1, inner_rows, 0)
        p0 = jnp.maximum(chunk - 1, 0)
        lax.fori_loop(p0 * (p0 + 3) // 2, chunk * (chunk + 3) // 2, inner1, 0)
        return 0

    lax.fori_loop(0, 3, chunk_step, 0)
    early_b = z_copy(b.at[2, :, 2], hb.at[2], 33, up)
    early_b.start()

    def end_a(g, _):
        for c in a_copies(g):
            c.wait()
        return 0

    lax.fori_loop(0, GROUPS, end_a, 0)
    fill_halo(ha, a, WIN, 4, (0, 9))

    def b_copies(e):
        part = pl.ds(10 * e, 10)
        return (
            z_copy(b.at[2, part, 1], hb.at[1, part], 27 + e, up),
            z_copy(b.at[2, part, 8], hb.at[0, part], 30 + e, down),
        )

    def edge1(e, _):
        conv1(5 * e, 5, EDGES)
        for c in b_copies(e):
            c.start()
        return 0

    lax.fori_loop(0, 3, edge1, 0)

    def inner2(i, _):
        conv2(7 * i, 7, INNER)
        return 0

    lax.fori_loop(0, 2, inner2, 0)

    def reduce_rows(rows):
        pieces = []
        for j2 in range(3):
            for k in range(3):
                tiles = []
                for j in range(14):
                    c = min(2 * j + k, OC - 1)
                    tiles += [ob[c, 2 * i + j2] for i in rows]
                pieces.append(jnp.concatenate(tiles, axis=0))
        acc = jnp.dot(jnp.concatenate(pieces, axis=1), rw[...], preferred_element_type=F32) + bias_r
        m = 16 * len(rows)
        for n, i in enumerate(rows):
            for jj in range(7):
                for h in range(2):
                    at = 2 * jj * m + 16 * n + 8 * h
                    e, o = acc[at : at + 8], acc[at + m : at + m + 8]
                    sb[2 * h, i, jj] = jnp.where(sub8 < 4, e, pltpu.roll(o, 4, 0)).astype(BF16)
                    sb[2 * h + 1, i, jj] = jnp.where(sub8 < 4, pltpu.roll(e, 4, 0), o).astype(BF16)

    slot = XB * core + x

    def out_copy(i, k):
        xb = (x + k // 2) % XB
        c = (core + k) % 2
        return pltpu.make_async_remote_copy(
            src_ref=sb.at[xb, i], dst_ref=gb.at[slot, y], send_sem=s_g.at[i, k], recv_sem=r_g.at[slot, y],
            device_id=(xb, z * YB + i, c), device_id_type=MESH,
        )

    def end_out(k, _):
        for i in range(4):

            @pl.when(jnp.logical_not(jnp.logical_and(k == 0, y == i)))
            def _():
                out_copy(i, k).wait_send()

        return 0

    def start_out(i):
        def step(k, _):
            here = jnp.logical_and(k == 0, y == i)

            @pl.when(jnp.logical_not(here))
            def _():
                out_copy(i, k).start()

            return 0

        lax.fori_loop(0, 8, step, 0)

    reduce_rows((1, 2))
    start_out(1)
    start_out(2)
    early_b.wait()

    def end_b(e, _):
        for c in b_copies(e):
            c.wait()
        return 0

    lax.fori_loop(0, 3, end_b, 0)
    fill_halo(hb, b, BC, 5, (0, 9, 10))

    def edge2(i, _):
        conv2(7 * i, 7, EDGES2)
        return 0

    lax.fori_loop(0, 2, edge2, 0)
    reduce_rows((0, 3))
    start_out(0)
    start_out(3)
    own_out = pltpu.make_async_copy(sb.at[x, y], gb.at[slot, y], l_a.at[1])
    own_out.start()
    own_out.wait()

    def wait_out(k, _):
        s, q = k // YB, k % YB

        @pl.when(jnp.logical_not(jnp.logical_and(s == slot, q == y)))
        def _():
            pltpu.make_async_remote_copy(
                src_ref=sb.at[0, 0], dst_ref=gb.at[s, q], send_sem=s_g.at[0, 0], recv_sem=r_g.at[s, q],
                device_id=(x, zy, 1 - core), device_id_type=MESH,
            ).wait_recv()

        return 0

    lax.fori_loop(0, 32, wait_out, 0)

    def select(s, _):
        src = jnp.int32(0)
        length = jnp.int32(0)
        for c in range(8):
            hit = owner[c] == XB * core + s
            src = jnp.where(hit, stored[c], src)
            length = jnp.where(hit, lengths[c], length)
        alive = (XB * x + sub8 % 4) < length
        columns = []
        for q in range(YB):
            tiles = gb[src, q]
            for j in range(JC):
                tile = tiles[j // 2].astype(F32)
                columns.append(tile if j % 2 == 0 else pltpu.roll(tile, 4, 0))
        for g in range(13):
            c0, c1, c2, c3 = columns[4 * g : 4 * g + 4]
            t1, t2, t3 = pltpu.roll(c1, 96, 1), pltpu.roll(c2, 64, 1), pltpu.roll(c3, 32, 1)
            dense = [jnp.where(lane < 96, c0, t1), jnp.where(lane < 64, t1, t2), jnp.where(lane < 32, t2, t3)]
            for m in range(3):
                out[s, :, pl.ds(384 * g + 128 * m, 128)] = jnp.where(alive, dense[m], 0.0)[0:4].astype(BF16)
        return 0

    lax.fori_loop(0, XB, select, 0)

    def end_in(chunk, _):
        for dx, dy in AROUND:
            in_copy(dx, dy, chunk).wait_send()
        return 0

    lax.fori_loop(0, 3, end_in, 0)
    lax.fori_loop(0, 8, end_out, 0)


def local(
    features, lengths, stored_slot, owner_slot, gain_first, conv_first, bias_first,
    gain_second, conv_second, bias_second, reduce_conv_weight, reduce_conv_bias,
):
    slots, frames, rows, lanes = features.shape
    feat = jnp.transpose(features, (0, 2, 1, 3)).reshape(slots, rows * frames, lanes)
    hbm = pl.BlockSpec(memory_space=pltpu.HBM)
    dma = pltpu.SemaphoreType.DMA
    result = pl.pallas_call(
        kernel,
        out_shape=jax.ShapeDtypeStruct((slots, frames, 4992), BF16),
        in_specs=[pl.BlockSpec(memory_space=pl.ANY)] + [hbm] * 11,
        out_specs=pl.BlockSpec(memory_space=pltpu.VMEM),
        scratch_shapes=[
            pltpu.VMEM((16, 8, WIN * CH), BF16),
            pltpu.VMEM((WIN, 9, 16, LANES), BF16),
            pltpu.VMEM((3, WIN, 10, 16, LANES), BF16),
            pltpu.VMEM((3, BC, 11, 16, LANES), BF16),
            pltpu.VMEM((9, 512, 256), BF16),
            pltpu.VMEM((9, 512, 256), BF16),
            pltpu.VMEM((1152, 128), BF16),
            pltpu.VMEM((OC, 9, 16, LANES), BF16),
            pltpu.VMEM((XB, 4, 7, 8, LANES), BF16),
            pltpu.VMEM((2 * XB, YB, 7, 8, LANES), BF16),
            pltpu.VMEM((2, WIN, 16, LANES), BF16),
            pltpu.VMEM((3, BC, 16, LANES), BF16),
            pltpu.VMEM((27, CH, CH), BF16),
            pltpu.VMEM((27, CH, CH), BF16),
            pltpu.VMEM((9, CH, CH), BF16),
            pltpu.VMEM((5, 1, CH), F32),
            pltpu.VMEM((8, LANES), F32),
            pltpu.VMEM((256, 256), BF16),
            pltpu.SMEM((8,), jnp.int32),
            pltpu.SMEM((8,), jnp.int32),
            pltpu.SMEM((8,), jnp.int32),
            dma((3, 16)),
            dma((3, 16)),
            dma((34,)),
            dma((34,)),
            dma((4, 8)),
            dma((8, 4)),
            dma((2,)),
            dma((11,)),
        ],
        compiler_params=pltpu.CompilerParams(
            collective_id=0, has_side_effects=True, vmem_limit_bytes=52 << 20
        ),
        name="encode",
    )(
        feat,
        conv_first.reshape(27, CH, CH),
        conv_second.reshape(27, CH, CH),
        reduce_conv_weight.reshape(9, CH, CH),
        *[v.reshape(1, CH) for v in (gain_first, bias_first, gain_second, bias_second, reduce_conv_bias)],
        lengths, stored_slot, owner_slot,
    )
    return result.reshape(slots, frames, 1, 4992)


def solution(mesh):
    spec = P("clip", "tm", "rows", None)
    return jax.shard_map(
        local, mesh=mesh, in_specs=(spec,) + (P(),) * 11, out_specs=spec, check_vma=False
    )
```

```python
import jax
import jax.numpy as jnp
from jax import lax
from jax.experimental import pallas as pl
from jax.experimental.pallas import tpu as pltpu
from jax.sharding import PartitionSpec as P

NORM_EPS = 1e-06
MESH = pl.DeviceIdType.MESH
F32 = jnp.float32
BF16 = jnp.bfloat16

CH = 96
XB = 4
YB = 4
ZB = 8
OWN = 26
GROUPS = 9
WIN = GROUPS * 4
LANES = 128
PAIRS1 = 15
PAIRS2 = 14
BC = 2 * PAIRS1
OC = 2 * PAIRS2
JC = 13


def shifted(flat, step, frame):
    return jnp.where(frame < step, 0.0, pltpu.roll(flat, step, 0))


def split_square(v):
    sq = v * v
    hi = sq.astype(BF16)
    return hi, (sq - hi.astype(F32)).astype(BF16)


def scaled_act(v, total, half_gain):
    half = v * lax.rsqrt(total * (1.0 / CH) + NORM_EPS) * half_gain
    return half + half * jnp.tanh(half)


def build_toeplitz(w_ref, wt):
    def tap(i, _):
        for n in range(2):
            for k in range(3):
                wt[i, pl.ds(128 * (n + k), CH), pl.ds(128 * n, CH)] = w_ref[3 * i + k]
        return 0

    lax.fori_loop(0, 9, tap, 0)


def conv_lhs(src, col0, pairs, rows):
    parts = []
    for t in range(3):
        for j in range(3):
            for k in range(4):
                pieces = []
                for p in range(pairs):
                    for first, count in rows:
                        block = src[t, col0 + 2 * p + k, first + j : first + j + count]
                        pieces.append(block.reshape(count * 16, LANES))
                parts.append(jnp.concatenate(pieces, axis=0))
    return jnp.concatenate(parts, axis=1)


INNER = ((1, 6),)
ORDER = (4, 5, 2, 6, 3, 7, 1, 0)
AROUND = sorted(
    ((dx, dy) for dx in range(4) for dy in range(4) if dx or dy),
    key=lambda d: -(min(d[0], 4 - d[0]) + min(d[1], 4 - d[1])),
)
EDGES = ((0, 1), (7, 1))
EDGES2 = ((0, 1), (7, 2))


def kernel(
    feat, w1h, w2h, wrh, g1h, b1h, g2h, b2h, brh, lenh, stoh, ownh, out,
    arr, xs, a, b, wt1, wt2, rw, ob, sb, gb, ha, hb, w1, w2, wr, vin, vec, ones2,
    lengths, stored, owner,
    s_a, r_a, s_z, r_z, s_g, r_g, l_a, l_w,
):
    x = lax.axis_index("tm")
    zy = lax.axis_index("rows")
    core = lax.axis_index("clip")
    z, y = zy // YB, zy % YB
    me = x * YB + y
    up = ((z + ZB - 1) % ZB) * YB + y
    down = ((z + 1) % ZB) * YB + y

    def plane(i):
        t = (me + i) % 16
        return t, (t // YB, z * YB + t % YB, core)

    def start_lane(q):
        return 2304 * q + 128 * (q // 2 - q // 3)

    def place(q):
        return 384 * (1 - (q + 3) // 4) + 128 * (q // 2 - q // 3)

    arr[:, :, 0:384] = jnp.zeros((16, 8, 384), BF16)
    arr[:, :, 3072:3456] = jnp.zeros((16, 8, 384), BF16)
    barrier = pltpu.get_barrier_semaphore()

    xs_of = [(x + d) % XB for d in range(XB)]
    ys_of = [(y + d) % YB for d in range(YB)]
    for dx in range(XB):
        for dy in range(YB):
            if dx or dy:
                dev = (xs_of[dx], z * YB + ys_of[dy], core)
                pl.semaphore_signal(barrier, inc=1, device_id=dev, device_id_type=MESH)
    for dev in ((x, up, core), (x, down, core), (x, zy, 1 - core)):
        pl.semaphore_signal(barrier, inc=1, device_id=dev, device_id_type=MESH)

    loads = [
        pltpu.make_async_copy(src, dst, l_w.at[i])
        for i, (src, dst) in enumerate(
            [(w1h, w1), (w2h, w2), (wrh, wr)]
            + [(v, vin.at[i]) for i, v in enumerate((g1h, b1h, g2h, b2h, brh))]
            + [(lenh, lengths), (stoh, stored), (ownh, owner)]
        )
    ]
    for c in loads:
        c.start()

    def zero_weights(i, _):
        wt1[i] = jnp.zeros((512, 256), BF16)
        wt2[i] = jnp.zeros((512, 256), BF16)
        return 0

    lax.fori_loop(0, 9, zero_weights, 0)
    rw[...] = jnp.zeros_like(rw)
    vec[...] = jnp.zeros_like(vec)
    r_i = lax.broadcasted_iota(jnp.int32, (256, 256), 0) // 128
    c_i = lax.broadcasted_iota(jnp.int32, (256, 256), 1) // 128
    ones2[...] = jnp.where(r_i == c_i, 1.0, 0.0).astype(BF16)
    loads[0].wait()
    build_toeplitz(w1, wt1)
    pl.semaphore_wait(barrier, 18)

    HALF = 1024

    starts = [start_lane(v) for v in ys_of]
    offs = [place(v) for v in ys_of]

    def in_copy(dx, dy, chunk):
        src = feat.at[xs_of[dx], :, pl.ds(pl.multiple_of(starts[dy] + HALF * chunk, 128), HALF)]
        dst = arr.at[me, :, pl.ds(pl.multiple_of(offs[dy] + HALF * chunk, 128), HALF)]
        return pltpu.make_async_remote_copy(
            src_ref=src, dst_ref=dst,
            send_sem=s_a.at[chunk, 4 * dx + dy],
            recv_sem=r_a.at[chunk, 4 * ((4 - dx) % 4) + (4 - dy) % 4],
            device_id=(xs_of[dx], z * YB + ys_of[dy], core), device_id_type=MESH,
        )

    my_off = place(y)
    own_in = pltpu.make_async_copy(
        feat.at[x, :, pl.ds(pl.multiple_of(start_lane(y), 128), 3 * HALF)],
        arr.at[me, :, pl.ds(pl.multiple_of(my_off, 128), 3 * HALF)],
        l_a.at[0],
    )
    own_in.start()

    def start_in(chunk, _):
        for dx, dy in AROUND:
            in_copy(dx, dy, chunk).start()
        return 0

    lax.fori_loop(0, 3, start_in, 0)

    for c in loads[1:]:
        c.wait()
    build_toeplitz(w2, wt2)

    def tap(i, _):
        rw[pl.ds(pl.multiple_of(128 * i, 128), CH), pl.ds(0, CH)] = wr[i]
        return 0

    lax.fori_loop(0, 9, tap, 0)
    for i in range(5):
        vec[i : i + 1, 0:CH] = vin[i]
    gain1, bias1, gain2, bias2, bias_r = [vec[i : i + 1] for i in range(5)]
    gain1, gain2 = 0.5 * gain1, 0.5 * gain2
    bias1w = jnp.concatenate([bias1, bias1], axis=1)
    gain2w = jnp.concatenate([gain2, gain2], axis=1)
    bias2w = jnp.concatenate([bias2, bias2], axis=1)

    own_in.wait()

    def wait_in(chunk):
        for dx, dy in AROUND:
            t = YB * xs_of[dx] + ys_of[dy]
            dst = arr.at[t, :, pl.ds(pl.multiple_of(my_off + HALF * chunk, 128), HALF)]
            pltpu.make_async_remote_copy(
                src_ref=feat.at[0, :, pl.ds(0, HALF)], dst_ref=dst,
                send_sem=s_a.at[chunk, 4 * dx + dy], recv_sem=r_a.at[chunk, 4 * dx + dy],
                device_id=(xs_of[dx], z * YB + ys_of[dy], core), device_id_type=MESH,
            ).wait_recv()

    lane = lax.broadcasted_iota(jnp.int32, (8, LANES), 1)
    sub8 = lax.broadcasted_iota(jnp.int32, (8, LANES), 0)
    ones1 = jnp.ones((256, LANES), BF16)
    frame128 = lax.broadcasted_iota(jnp.int32, (128, LANES), 0) % 16

    def act_group(q, g):
        lane0 = pl.multiple_of(g * 384, 128)
        cols = [[] for _ in range(4)]
        for xb in range(XB):
            v = [arr[XB * xb + q, :, pl.ds(lane0 + 128 * m, 128)].astype(F32) for m in range(3)]
            cols[0].append(jnp.where(lane < 96, v[0], 0.0))
            cols[1].append(
                jnp.where(lane < 32, pltpu.roll(v[0], 32, 1), jnp.where(lane < 96, pltpu.roll(v[1], 32, 1), 0.0))
            )
            cols[2].append(
                jnp.where(lane < 64, pltpu.roll(v[1], 64, 1), jnp.where(lane < 96, pltpu.roll(v[2], 64, 1), 0.0))
            )
            cols[3].append(jnp.where(lane < 96, pltpu.roll(v[2], 96, 1), 0.0))
        tiles = []
        for c in cols:
            turned = [pltpu.roll(u, 4, 0) for u in c]
            tiles += [jnp.where(sub8 < 4, c[0], turned[1]), jnp.where(sub8 < 4, c[2], turned[3])]
            tiles += [jnp.where(sub8 < 4, turned[0], c[1]), jnp.where(sub8 < 4, turned[2], c[3])]
        return jnp.concatenate(tiles, axis=0)

    def act_store(flat, total, q, g):
        w0 = 4 * g
        row = 2 * q
        xs[pl.ds(w0, 4), pl.ds(row, 2)] = flat.astype(BF16).reshape(4, 2, 16, LANES)
        act = scaled_act(flat, total, gain1)
        for t in range(3):
            moved = act if t == 2 else shifted(act, 2 - t, frame128)
            a[t, pl.ds(w0, 4), pl.ds(row + 1, 2)] = moved.astype(BF16).reshape(4, 2, 16, LANES)

    def act_step(i, qs):
        flats = [act_group(q, i) for q in qs]
        hi, lo = split_square(jnp.concatenate(flats, axis=0))
        total = jnp.dot(jnp.concatenate([hi, lo], axis=1), ones1, preferred_element_type=F32)
        for m, q in enumerate(qs):
            act_store(flats[m], total[128 * m : 128 * m + 128], q, i)
        return 0

    def z_copy(src, dst, k, row):
        return pltpu.make_async_remote_copy(
            src_ref=src, dst_ref=dst, send_sem=s_z.at[k], recv_sem=r_z.at[k],
            device_id=(x, row, core), device_id_type=MESH,
        )

    inside = (z > 0, z < ZB - 1)

    def fill_halo(halo, dst, count, unit, sides):
        frame = lax.broadcasted_iota(jnp.int32, (16 * unit, LANES), 0) % 16

        def step(i, _):
            c = unit * i
            for side, row in enumerate(sides):
                v = halo[side, pl.ds(c, unit)].astype(F32).reshape(16 * unit, LANES)
                v = jnp.where(inside[min(side, 1)], v, 0.0)
                for t in range(3):
                    moved = v if t == 2 else shifted(v, 2 - t, frame)
                    dst[t, pl.ds(c, unit), row] = moved.astype(BF16).reshape(unit, 16, LANES)
            return 0

        lax.fori_loop(0, count // unit, step, 0)

    base = 2 * (1 - y % 2) + 4 * (y // 3)
    col0 = OWN * y

    def conv1(p0, pairs, rows):
        acc = jnp.dot(
            conv_lhs(a, base + 2 * p0, pairs, rows), wt1[...].reshape(4608, 256), preferred_element_type=F32
        )
        v = acc + bias1w
        hi, lo = split_square(v)
        total = jnp.dot(hi, ones2[...], preferred_element_type=F32) + jnp.dot(
            lo, ones2[...], preferred_element_type=F32
        )
        act = scaled_act(v, total, gain2w)
        height = sum(count for _, count in rows)
        m = 16 * height
        frame = lax.broadcasted_iota(jnp.int32, (m, LANES), 0) % 16
        for p in range(pairs):
            for n in range(2):
                bcol = 2 * (p0 + p) + n
                image = col0 - 1 + bcol
                u = act[m * p : m * p + m, 128 * n : 128 * n + 128]
                u = jnp.where(jnp.logical_and(image >= 0, image < 104), u, 0.0)
                for t in range(3):
                    moved = (u if t == 2 else shifted(u, 2 - t, frame)).astype(BF16)
                    at = 0
                    for first, count in rows:
                        b[t, bcol, first + 1 : first + 1 + count] = moved[16 * at : 16 * (at + count)].reshape(
                            count, 16, LANES
                        )
                        at += count

    def conv2(p0, pairs, rows):
        acc = jnp.dot(
            conv_lhs(b, 2 * p0, pairs, rows), wt2[...].reshape(4608, 256), preferred_element_type=F32
        )
        v = acc + bias2w
        height = sum(count for _, count in rows)
        m = 16 * height
        for p in range(pairs):
            for n in range(2):
                c = 2 * (p0 + p) + n
                u = v[m * p : m * p + m, 128 * n : 128 * n + 128]
                at = 0
                for first, count in rows:
                    part = u[16 * at : 16 * (at + count)]
                    part = part + xs[base + 2 + c, first : first + count].reshape(16 * count, LANES).astype(F32)
                    part = jnp.where(col0 + c < 104, part, 0.0).astype(BF16).reshape(count, 16, LANES)
                    if first + count == 9:
                        ob[c, first : first + count - 1] = part[: count - 1]
                        ob[c, 8:9] = jnp.where(z < ZB - 1, part[count - 1 :], 0.0).astype(BF16)
                    else:
                        ob[c, first : first + count] = part
                    at += count

    def inner1(i, _):
        conv1(3 * i, 3, INNER)
        return 0

    def a_copies(g):
        part = pl.ds(4 * g, 4)
        return (
            z_copy(a.at[2, part, 1], ha.at[1, part], g, up),
            z_copy(a.at[2, part, 8], ha.at[0, part], 9 + g, down),
            z_copy(xs.at[part, 0], xs.at[part, 8], 18 + g, up),
        )

    def outer_rows(g, _):
        act_step(g, (0, 3))
        for c in a_copies(g):
            c.start()
        return 0

    def inner_rows(g, _):
        return act_step(g, (1, 2))

    def chunk_step(chunk, _):
        wait_in(chunk)
        g0, g1 = chunk * (chunk + 3) // 2, (chunk + 1) * (chunk + 4) // 2
        lax.fori_loop(g0, g1, outer_rows, 0)
        lax.fori_loop(g0, g1, inner_rows, 0)
        p0 = jnp.maximum(chunk - 1, 0)
        lax.fori_loop(p0 * (p0 + 3) // 2, chunk * (chunk + 3) // 2, inner1, 0)
        return 0

    lax.fori_loop(0, 3, chunk_step, 0)
    early_b = z_copy(b.at[2, :, 2], hb.at[2], 33, up)
    early_b.start()

    def got_a(g, _):
        for c in a_copies(g)[:2]:
            c.wait_recv()
        return 0

    lax.fori_loop(0, GROUPS, got_a, 0)
    fill_halo(ha, a, WIN, 4, (0, 9))

    def b_copies(e):
        part = pl.ds(10 * e, 10)
        return (
            z_copy(b.at[2, part, 1], hb.at[1, part], 27 + e, up),
            z_copy(b.at[2, part, 8], hb.at[0, part], 30 + e, down),
        )

    def edge1(e, _):
        conv1(5 * e, 5, EDGES)
        for c in b_copies(e):
            c.start()
        return 0

    lax.fori_loop(0, 3, edge1, 0)

    def inner2(i, _):
        conv2(7 * i, 7, INNER)
        return 0

    lax.fori_loop(0, 2, inner2, 0)

    def reduce_rows(rows):
        pieces = []
        for j2 in range(3):
            for k in range(3):
                tiles = []
                for j in range(14):
                    c = min(2 * j + k, OC - 1)
                    tiles += [ob[c, 2 * i + j2] for i in rows]
                pieces.append(jnp.concatenate(tiles, axis=0))
        acc = jnp.dot(jnp.concatenate(pieces, axis=1), rw[...], preferred_element_type=F32) + bias_r
        m = 16 * len(rows)
        for n, i in enumerate(rows):
            for jj in range(7):
                for h in range(2):
                    at = 2 * jj * m + 16 * n + 8 * h
                    e, o = acc[at : at + 8], acc[at + m : at + m + 8]
                    sb[2 * h, i, jj] = jnp.where(sub8 < 4, e, pltpu.roll(o, 4, 0)).astype(BF16)
                    sb[2 * h + 1, i, jj] = jnp.where(sub8 < 4, pltpu.roll(e, 4, 0), o).astype(BF16)

    slot = XB * core + x

    def out_copy(i, k):
        xb = xs_of[ORDER[k] // 2]
        c = core if ORDER[k] % 2 == 0 else 1 - core
        return pltpu.make_async_remote_copy(
            src_ref=sb.at[xb, i], dst_ref=gb.at[slot, y], send_sem=s_g.at[i, k], recv_sem=r_g.at[slot, y],
            device_id=(xb, z * YB + i, c), device_id_type=MESH,
        )

    def each_out(i, act):
        for k in range(8):
            if ORDER[k]:
                act(out_copy(i, k))
            else:

                @pl.when(y != i)
                def _():
                    act(out_copy(i, k))

    def start_out(i):
        each_out(i, lambda c: c.start())

    reduce_rows((1, 2))
    start_out(1)
    start_out(2)
    early_b.wait_recv()

    def got_b(e, _):
        for c in b_copies(e):
            c.wait_recv()
        return 0

    lax.fori_loop(0, 3, got_b, 0)

    def got_x(g, _):
        a_copies(g)[2].wait_recv()
        return 0

    lax.fori_loop(0, GROUPS, got_x, 0)
    fill_halo(hb, b, BC, 5, (0, 9, 10))

    def edge2(i, _):
        conv2(7 * i, 7, EDGES2)
        return 0

    lax.fori_loop(0, 2, edge2, 0)
    reduce_rows((0, 3))
    start_out(0)
    start_out(3)
    own_out = pltpu.make_async_copy(sb.at[x, y], gb.at[slot, y], l_a.at[1])
    own_out.start()
    own_out.wait()

    def wait_out(k, _):
        s, q = k // YB, k % YB

        @pl.when(jnp.logical_not(jnp.logical_and(s == slot, q == y)))
        def _():
            pltpu.make_async_remote_copy(
                src_ref=sb.at[0, 0], dst_ref=gb.at[s, q], send_sem=s_g.at[0, 0], recv_sem=r_g.at[s, q],
                device_id=(x, zy, 1 - core), device_id_type=MESH,
            ).wait_recv()

        return 0

    def end_in(chunk, _):
        for dx, dy in AROUND:
            in_copy(dx, dy, chunk).wait_send()
        return 0

    lax.fori_loop(0, 3, end_in, 0)
    for i in range(4):
        each_out(i, lambda c: c.wait_send())

    def end_rows(g, _):
        for c in a_copies(g):
            c.wait_send()
        return 0

    lax.fori_loop(0, GROUPS, end_rows, 0)

    def end_b(e, _):
        for c in b_copies(e):
            c.wait_send()
        return 0

    lax.fori_loop(0, 3, end_b, 0)
    early_b.wait_send()
    lax.fori_loop(0, 32, wait_out, 0)

    def select(s, _):
        src = jnp.int32(0)
        length = jnp.int32(0)
        for c in range(8):
            hit = owner[c] == XB * core + s
            src = jnp.where(hit, stored[c], src)
            length = jnp.where(hit, lengths[c], length)
        alive = (XB * x + sub8 % 4) < length
        columns = []
        for q in range(YB):
            tiles = gb[src, q]
            for j in range(JC):
                tile = tiles[j // 2].astype(F32)
                columns.append(tile if j % 2 == 0 else pltpu.roll(tile, 4, 0))
        for g in range(13):
            c0, c1, c2, c3 = columns[4 * g : 4 * g + 4]
            t1, t2, t3 = pltpu.roll(c1, 96, 1), pltpu.roll(c2, 64, 1), pltpu.roll(c3, 32, 1)
            dense = [jnp.where(lane < 96, c0, t1), jnp.where(lane < 64, t1, t2), jnp.where(lane < 32, t2, t3)]
            for m in range(3):
                out[s, :, pl.ds(384 * g + 128 * m, 128)] = jnp.where(alive, dense[m], 0.0)[0:4].astype(BF16)
        return 0

    lax.fori_loop(0, XB, select, 0)


def local(
    features, lengths, stored_slot, owner_slot, gain_first, conv_first, bias_first,
    gain_second, conv_second, bias_second, reduce_conv_weight, reduce_conv_bias,
):
    slots, frames, rows, lanes = features.shape
    feat = jnp.transpose(features, (0, 2, 1, 3)).reshape(slots, rows * frames, lanes)
    hbm = pl.BlockSpec(memory_space=pltpu.HBM)
    dma = pltpu.SemaphoreType.DMA
    result = pl.pallas_call(
        kernel,
        out_shape=jax.ShapeDtypeStruct((slots, frames, 4992), BF16),
        in_specs=[pl.BlockSpec(memory_space=pl.ANY)] + [hbm] * 11,
        out_specs=pl.BlockSpec(memory_space=pltpu.VMEM),
        scratch_shapes=[
            pltpu.VMEM((16, 8, WIN * CH), BF16),
            pltpu.VMEM((WIN, 9, 16, LANES), BF16),
            pltpu.VMEM((3, WIN, 10, 16, LANES), BF16),
            pltpu.VMEM((3, BC, 11, 16, LANES), BF16),
            pltpu.VMEM((9, 512, 256), BF16),
            pltpu.VMEM((9, 512, 256), BF16),
            pltpu.VMEM((1152, 128), BF16),
            pltpu.VMEM((OC, 9, 16, LANES), BF16),
            pltpu.VMEM((XB, 4, 7, 8, LANES), BF16),
            pltpu.VMEM((2 * XB, YB, 7, 8, LANES), BF16),
            pltpu.VMEM((2, WIN, 16, LANES), BF16),
            pltpu.VMEM((3, BC, 16, LANES), BF16),
            pltpu.VMEM((27, CH, CH), BF16),
            pltpu.VMEM((27, CH, CH), BF16),
            pltpu.VMEM((9, CH, CH), BF16),
            pltpu.VMEM((5, 1, CH), F32),
            pltpu.VMEM((8, LANES), F32),
            pltpu.VMEM((256, 256), BF16),
            pltpu.SMEM((8,), jnp.int32),
            pltpu.SMEM((8,), jnp.int32),
            pltpu.SMEM((8,), jnp.int32),
            dma((3, 16)),
            dma((3, 16)),
            dma((34,)),
            dma((34,)),
            dma((4, 8)),
            dma((8, 4)),
            dma((2,)),
            dma((11,)),
        ],
        compiler_params=pltpu.CompilerParams(
            collective_id=0, has_side_effects=True, vmem_limit_bytes=52 << 20
        ),
        name="encode",
    )(
        feat,
        conv_first.reshape(27, CH, CH),
        conv_second.reshape(27, CH, CH),
        reduce_conv_weight.reshape(9, CH, CH),
        *[v.reshape(1, CH) for v in (gain_first, bias_first, gain_second, bias_second, reduce_conv_bias)],
        lengths, stored_slot, owner_slot,
    )
    return result.reshape(slots, frames, 1, 4992)


def solution(mesh):
    spec = P("clip", "tm", "rows", None)
    return jax.shard_map(
        local, mesh=mesh, in_specs=(spec,) + (P(),) * 11, out_specs=spec, check_vma=False
    )
```

```python
import jax
import jax.numpy as jnp
from jax import lax
from jax.experimental import pallas as pl
from jax.experimental.pallas import tpu as pltpu
from jax.sharding import PartitionSpec as P

NORM_EPS = 1e-06
MESH = pl.DeviceIdType.MESH
F32 = jnp.float32
BF16 = jnp.bfloat16

CH = 96
XB = 4
YB = 4
ZB = 8
OWN = 26
GROUPS = 9
WIN = GROUPS * 4
LANES = 128
PAIRS1 = 15
PAIRS2 = 14
BC = 2 * PAIRS1
OC = 2 * PAIRS2
JC = 13


def shifted(flat, step, frame):
    return jnp.where(frame < step, 0.0, pltpu.roll(flat, step, 0))


def split_square(v):
    sq = v * v
    hi = sq.astype(BF16)
    return hi, (sq - hi.astype(F32)).astype(BF16)


def scaled_act(v, total, half_gain):
    half = v * lax.rsqrt(total * (1.0 / CH) + NORM_EPS) * half_gain
    return half + half * jnp.tanh(half)


def build_toeplitz(w_ref, wt):
    def tap(i, _):
        for n in range(2):
            for k in range(3):
                wt[i, pl.ds(128 * (n + k), CH), pl.ds(128 * n, CH)] = w_ref[3 * i + k]
        return 0

    lax.fori_loop(0, 9, tap, 0)


def conv_lhs(src, col0, pairs, rows):
    parts = []
    for t in range(3):
        for j in range(3):
            for k in range(4):
                pieces = []
                for p in range(pairs):
                    for first, count in rows:
                        block = src[t, col0 + 2 * p + k, first + j : first + j + count]
                        pieces.append(block.reshape(count * 16, LANES))
                parts.append(jnp.concatenate(pieces, axis=0))
    return jnp.concatenate(parts, axis=1)


INNER = ((1, 6),)
ORDER = (4, 5, 2, 6, 3, 7, 1, 0)
AROUND = sorted(
    ((dx, dy) for dx in range(4) for dy in range(4) if dx or dy),
    key=lambda d: -(min(d[0], 4 - d[0]) + min(d[1], 4 - d[1])),
)
EDGES = ((0, 1), (7, 1))
EDGES2 = ((0, 1), (7, 2))


def kernel(
    feat, w1h, w2h, wrh, g1h, b1h, g2h, b2h, brh, lenh, stoh, ownh, out,
    arr, xs, a, b, wt1, wt2, rw, ob, sb, gb, ha, hb, w1, w2, wr, vin, vec, ones2,
    lengths, stored, owner,
    s_a, r_a, s_z, r_z, s_g, r_g, l_a, l_w,
):
    x = lax.axis_index("tm")
    zy = lax.axis_index("rows")
    core = lax.axis_index("clip")
    z, y = zy // YB, zy % YB
    me = x * YB + y
    up = ((z + ZB - 1) % ZB) * YB + y
    down = ((z + 1) % ZB) * YB + y

    def plane(i):
        t = (me + i) % 16
        return t, (t // YB, z * YB + t % YB, core)

    def start_lane(q):
        return 2304 * q + 128 * (q // 2 - q // 3)

    def place(q):
        return 384 * (1 - (q + 3) // 4) + 128 * (q // 2 - q // 3)

    arr[:, :, 0:384] = jnp.zeros((16, 8, 384), BF16)
    arr[:, :, 3072:3456] = jnp.zeros((16, 8, 384), BF16)
    barrier = pltpu.get_barrier_semaphore()

    xs_of = [(x + d) % XB for d in range(XB)]
    ys_of = [(y + d) % YB for d in range(YB)]
    for dx in range(XB):
        for dy in range(YB):
            if dx or dy:
                dev = (xs_of[dx], z * YB + ys_of[dy], core)
                pl.semaphore_signal(barrier, inc=1, device_id=dev, device_id_type=MESH)
    for dev in ((x, up, core), (x, down, core), (x, zy, 1 - core)):
        pl.semaphore_signal(barrier, inc=1, device_id=dev, device_id_type=MESH)

    loads = [
        pltpu.make_async_copy(src, dst, l_w.at[i])
        for i, (src, dst) in enumerate(
            [(w1h, w1), (w2h, w2), (wrh, wr)]
            + [(v, vin.at[i]) for i, v in enumerate((g1h, b1h, g2h, b2h, brh))]
            + [(lenh, lengths), (stoh, stored), (ownh, owner)]
        )
    ]
    for c in loads:
        c.start()

    def zero_weights(i, _):
        wt1[i] = jnp.zeros((512, 256), BF16)
        wt2[i] = jnp.zeros((512, 256), BF16)
        return 0

    lax.fori_loop(0, 9, zero_weights, 0)
    rw[...] = jnp.zeros_like(rw)
    vec[...] = jnp.zeros_like(vec)
    r_i = lax.broadcasted_iota(jnp.int32, (256, 256), 0) // 128
    c_i = lax.broadcasted_iota(jnp.int32, (256, 256), 1) // 128
    ones2[...] = jnp.where(r_i == c_i, 1.0, 0.0).astype(BF16)
    loads[0].wait()
    build_toeplitz(w1, wt1)
    pl.semaphore_wait(barrier, 18)

    HALF = 1024

    starts = [start_lane(v) for v in ys_of]
    offs = [place(v) for v in ys_of]

    def in_copy(dx, dy, chunk):
        src = feat.at[xs_of[dx], :, pl.ds(pl.multiple_of(starts[dy] + HALF * chunk, 128), HALF)]
        dst = arr.at[me, :, pl.ds(pl.multiple_of(offs[dy] + HALF * chunk, 128), HALF)]
        return pltpu.make_async_remote_copy(
            src_ref=src, dst_ref=dst,
            send_sem=s_a.at[chunk, 4 * dx + dy],
            recv_sem=r_a.at[chunk, 4 * ((4 - dx) % 4) + (4 - dy) % 4],
            device_id=(xs_of[dx], z * YB + ys_of[dy], core), device_id_type=MESH,
        )

    my_off = place(y)
    own_in = pltpu.make_async_copy(
        feat.at[x, :, pl.ds(pl.multiple_of(start_lane(y), 128), 3 * HALF)],
        arr.at[me, :, pl.ds(pl.multiple_of(my_off, 128), 3 * HALF)],
        l_a.at[0],
    )
    own_in.start()

    def start_in(chunk, _):
        for dx, dy in AROUND:
            in_copy(dx, dy, chunk).start()
        return 0

    lax.fori_loop(0, 3, start_in, 0)

    for c in loads[1:]:
        c.wait()
    build_toeplitz(w2, wt2)

    def tap(i, _):
        rw[pl.ds(pl.multiple_of(128 * i, 128), CH), pl.ds(0, CH)] = wr[i]
        return 0

    lax.fori_loop(0, 9, tap, 0)
    for i in range(5):
        vec[i : i + 1, 0:CH] = vin[i]
    gain1, bias1, gain2, bias2, bias_r = [vec[i : i + 1] for i in range(5)]
    gain1, gain2 = 0.5 * gain1, 0.5 * gain2
    bias1w = jnp.concatenate([bias1, bias1], axis=1)
    gain2w = jnp.concatenate([gain2, gain2], axis=1)
    bias2w = jnp.concatenate([bias2, bias2], axis=1)

    own_in.wait()

    def wait_in(chunk):
        for dx, dy in AROUND:
            t = YB * xs_of[dx] + ys_of[dy]
            dst = arr.at[t, :, pl.ds(pl.multiple_of(my_off + HALF * chunk, 128), HALF)]
            pltpu.make_async_remote_copy(
                src_ref=feat.at[0, :, pl.ds(0, HALF)], dst_ref=dst,
                send_sem=s_a.at[chunk, 4 * dx + dy], recv_sem=r_a.at[chunk, 4 * dx + dy],
                device_id=(xs_of[dx], z * YB + ys_of[dy], core), device_id_type=MESH,
            ).wait_recv()

    lane = lax.broadcasted_iota(jnp.int32, (8, LANES), 1)
    sub8 = lax.broadcasted_iota(jnp.int32, (8, LANES), 0)
    ones1 = jnp.ones((256, LANES), BF16)
    frame128 = lax.broadcasted_iota(jnp.int32, (128, LANES), 0) % 16

    def act_group(q, g):
        lane0 = pl.multiple_of(g * 384, 128)
        cols = [[] for _ in range(4)]
        for xb in range(XB):
            v = [arr[XB * xb + q, :, pl.ds(lane0 + 128 * m, 128)].astype(F32) for m in range(3)]
            cols[0].append(jnp.where(lane < 96, v[0], 0.0))
            cols[1].append(
                jnp.where(lane < 32, pltpu.roll(v[0], 32, 1), jnp.where(lane < 96, pltpu.roll(v[1], 32, 1), 0.0))
            )
            cols[2].append(
                jnp.where(lane < 64, pltpu.roll(v[1], 64, 1), jnp.where(lane < 96, pltpu.roll(v[2], 64, 1), 0.0))
            )
            cols[3].append(jnp.where(lane < 96, pltpu.roll(v[2], 96, 1), 0.0))
        tiles = []
        for c in cols:
            turned = [pltpu.roll(u, 4, 0) for u in c]
            tiles += [jnp.where(sub8 < 4, c[0], turned[1]), jnp.where(sub8 < 4, c[2], turned[3])]
            tiles += [jnp.where(sub8 < 4, turned[0], c[1]), jnp.where(sub8 < 4, turned[2], c[3])]
        return jnp.concatenate(tiles, axis=0)

    def act_store(flat, total, q, g):
        w0 = 4 * g
        row = 2 * q
        xs[pl.ds(w0, 4), pl.ds(row, 2)] = flat.astype(BF16).reshape(4, 2, 16, LANES)
        act = scaled_act(flat, total, gain1)
        for t in range(3):
            moved = act if t == 2 else shifted(act, 2 - t, frame128)
            a[t, pl.ds(w0, 4), pl.ds(row + 1, 2)] = moved.astype(BF16).reshape(4, 2, 16, LANES)

    def act_step(i, qs):
        flats = [act_group(q, i) for q in qs]
        hi, lo = split_square(jnp.concatenate(flats, axis=0))
        total = jnp.dot(jnp.concatenate([hi, lo], axis=1), ones1, preferred_element_type=F32)
        for m, q in enumerate(qs):
            act_store(flats[m], total[128 * m : 128 * m + 128], q, i)
        return 0

    def z_copy(src, dst, k, row):
        return pltpu.make_async_remote_copy(
            src_ref=src, dst_ref=dst, send_sem=s_z.at[k], recv_sem=r_z.at[k],
            device_id=(x, row, core), device_id_type=MESH,
        )

    inside = (z > 0, z < ZB - 1)

    def fill_halo(halo, dst, count, unit, sides):
        frame = lax.broadcasted_iota(jnp.int32, (16 * unit, LANES), 0) % 16

        def step(i, _):
            c = unit * i
            for side, row in enumerate(sides):
                v = halo[side, pl.ds(c, unit)].astype(F32).reshape(16 * unit, LANES)
                v = jnp.where(inside[min(side, 1)], v, 0.0)
                for t in range(3):
                    moved = v if t == 2 else shifted(v, 2 - t, frame)
                    dst[t, pl.ds(c, unit), row] = moved.astype(BF16).reshape(unit, 16, LANES)
            return 0

        lax.fori_loop(0, count // unit, step, 0)

    base = 2 * (1 - y % 2) + 4 * (y // 3)
    col0 = OWN * y

    def conv1(p0, pairs, rows):
        acc = jnp.dot(
            conv_lhs(a, base + 2 * p0, pairs, rows), wt1[...].reshape(4608, 256), preferred_element_type=F32
        )
        v = acc + bias1w
        hi, lo = split_square(v)
        total = jnp.dot(hi, ones2[...], preferred_element_type=F32) + jnp.dot(
            lo, ones2[...], preferred_element_type=F32
        )
        act = scaled_act(v, total, gain2w)
        height = sum(count for _, count in rows)
        m = 16 * height
        frame = lax.broadcasted_iota(jnp.int32, (m, LANES), 0) % 16
        for p in range(pairs):
            for n in range(2):
                bcol = 2 * (p0 + p) + n
                image = col0 - 1 + bcol
                u = act[m * p : m * p + m, 128 * n : 128 * n + 128]
                u = jnp.where(jnp.logical_and(image >= 0, image < 104), u, 0.0)
                for t in range(3):
                    moved = (u if t == 2 else shifted(u, 2 - t, frame)).astype(BF16)
                    at = 0
                    for first, count in rows:
                        b[t, bcol, first + 1 : first + 1 + count] = moved[16 * at : 16 * (at + count)].reshape(
                            count, 16, LANES
                        )
                        at += count

    def conv2(p0, pairs, rows):
        acc = jnp.dot(
            conv_lhs(b, 2 * p0, pairs, rows), wt2[...].reshape(4608, 256), preferred_element_type=F32
        )
        v = acc + bias2w
        height = sum(count for _, count in rows)
        m = 16 * height
        for p in range(pairs):
            for n in range(2):
                c = 2 * (p0 + p) + n
                u = v[m * p : m * p + m, 128 * n : 128 * n + 128]
                at = 0
                for first, count in rows:
                    part = u[16 * at : 16 * (at + count)]
                    part = part + xs[base + 2 + c, first : first + count].reshape(16 * count, LANES).astype(F32)
                    part = jnp.where(col0 + c < 104, part, 0.0).astype(BF16).reshape(count, 16, LANES)
                    if first + count == 9:
                        ob[c, first : first + count - 1] = part[: count - 1]
                        ob[c, 8:9] = jnp.where(z < ZB - 1, part[count - 1 :], 0.0).astype(BF16)
                    else:
                        ob[c, first : first + count] = part
                    at += count

    def inner1(i, _):
        conv1(3 * i, 3, INNER)
        return 0

    def a_copies(g):
        part = pl.ds(4 * g, 4)
        return (
            z_copy(a.at[2, part, 1], ha.at[1, part], g, up),
            z_copy(a.at[2, part, 8], ha.at[0, part], 9 + g, down),
            z_copy(xs.at[part, 0], xs.at[part, 8], 18 + g, up),
        )

    def all_rows(g, _):
        act_step(g, (0, 1, 2, 3))
        for c in a_copies(g):
            c.start()
        return 0

    def chunk_step(chunk, _):
        wait_in(chunk)
        g0, g1 = chunk * (chunk + 3) // 2, (chunk + 1) * (chunk + 4) // 2
        lax.fori_loop(g0, g1, all_rows, 0)
        p0 = jnp.maximum(chunk - 1, 0)
        lax.fori_loop(p0 * (p0 + 3) // 2, chunk * (chunk + 3) // 2, inner1, 0)
        return 0

    lax.fori_loop(0, 3, chunk_step, 0)
    early_b = z_copy(b.at[2, :, 2], hb.at[2], 33, up)
    early_b.start()

    def got_a(g, _):
        for c in a_copies(g)[:2]:
            c.wait_recv()
        return 0

    lax.fori_loop(0, GROUPS, got_a, 0)
    fill_halo(ha, a, WIN, 4, (0, 9))

    def b_copies(e):
        part = pl.ds(10 * e, 10)
        return (
            z_copy(b.at[2, part, 1], hb.at[1, part], 27 + e, up),
            z_copy(b.at[2, part, 8], hb.at[0, part], 30 + e, down),
        )

    def edge1(e, _):
        conv1(5 * e, 5, EDGES)
        for c in b_copies(e):
            c.start()
        return 0

    lax.fori_loop(0, 3, edge1, 0)

    def inner2(i, _):
        conv2(7 * i, 7, INNER)
        return 0

    lax.fori_loop(0, 2, inner2, 0)

    def reduce_rows(rows):
        pieces = []
        for j2 in range(3):
            for k in range(3):
                tiles = []
                for j in range(14):
                    c = min(2 * j + k, OC - 1)
                    tiles += [ob[c, 2 * i + j2] for i in rows]
                pieces.append(jnp.concatenate(tiles, axis=0))
        acc = jnp.dot(jnp.concatenate(pieces, axis=1), rw[...], preferred_element_type=F32) + bias_r
        m = 16 * len(rows)
        for n, i in enumerate(rows):
            for jj in range(7):
                for h in range(2):
                    at = 2 * jj * m + 16 * n + 8 * h
                    e, o = acc[at : at + 8], acc[at + m : at + m + 8]
                    sb[2 * h, i, jj] = jnp.where(sub8 < 4, e, pltpu.roll(o, 4, 0)).astype(BF16)
                    sb[2 * h + 1, i, jj] = jnp.where(sub8 < 4, pltpu.roll(e, 4, 0), o).astype(BF16)

    slot = XB * core + x

    def out_copy(i, k):
        xb = xs_of[ORDER[k] // 2]
        c = core if ORDER[k] % 2 == 0 else 1 - core
        return pltpu.make_async_remote_copy(
            src_ref=sb.at[xb, i], dst_ref=gb.at[slot, y], send_sem=s_g.at[i, k], recv_sem=r_g.at[slot, y],
            device_id=(xb, z * YB + i, c), device_id_type=MESH,
        )

    def each_out(i, act):
        for k in range(8):
            if ORDER[k]:
                act(out_copy(i, k))
            else:

                @pl.when(y != i)
                def _():
                    act(out_copy(i, k))

    def start_out(i):
        each_out(i, lambda c: c.start())

    reduce_rows((1, 2))
    start_out(1)
    start_out(2)
    early_b.wait_recv()

    def got_b(e, _):
        for c in b_copies(e):
            c.wait_recv()
        return 0

    lax.fori_loop(0, 3, got_b, 0)

    def got_x(g, _):
        a_copies(g)[2].wait_recv()
        return 0

    lax.fori_loop(0, GROUPS, got_x, 0)
    fill_halo(hb, b, BC, 5, (0, 9, 10))

    def edge2(i, _):
        conv2(7 * i, 7, EDGES2)
        return 0

    lax.fori_loop(0, 2, edge2, 0)
    reduce_rows((0, 3))
    start_out(0)
    start_out(3)
    own_out = pltpu.make_async_copy(sb.at[x, y], gb.at[slot, y], l_a.at[1])
    own_out.start()
    own_out.wait()

    def wait_out(k, _):
        s, q = k // YB, k % YB

        @pl.when(jnp.logical_not(jnp.logical_and(s == slot, q == y)))
        def _():
            pltpu.make_async_remote_copy(
                src_ref=sb.at[0, 0], dst_ref=gb.at[s, q], send_sem=s_g.at[0, 0], recv_sem=r_g.at[s, q],
                device_id=(x, zy, 1 - core), device_id_type=MESH,
            ).wait_recv()

        return 0

    def end_in(chunk, _):
        for dx, dy in AROUND:
            in_copy(dx, dy, chunk).wait_send()
        return 0

    lax.fori_loop(0, 3, end_in, 0)
    for i in range(4):
        each_out(i, lambda c: c.wait_send())

    def end_rows(g, _):
        for c in a_copies(g):
            c.wait_send()
        return 0

    lax.fori_loop(0, GROUPS, end_rows, 0)

    def end_b(e, _):
        for c in b_copies(e):
            c.wait_send()
        return 0

    lax.fori_loop(0, 3, end_b, 0)
    early_b.wait_send()
    lax.fori_loop(0, 32, wait_out, 0)

    def select(s, _):
        src = jnp.int32(0)
        length = jnp.int32(0)
        for c in range(8):
            hit = owner[c] == XB * core + s
            src = jnp.where(hit, stored[c], src)
            length = jnp.where(hit, lengths[c], length)
        alive = (XB * x + sub8 % 4) < length
        columns = []
        for q in range(YB):
            tiles = gb[src, q]
            for j in range(JC):
                tile = tiles[j // 2].astype(F32)
                columns.append(tile if j % 2 == 0 else pltpu.roll(tile, 4, 0))
        for g in range(13):
            c0, c1, c2, c3 = columns[4 * g : 4 * g + 4]
            t1, t2, t3 = pltpu.roll(c1, 96, 1), pltpu.roll(c2, 64, 1), pltpu.roll(c3, 32, 1)
            dense = [jnp.where(lane < 96, c0, t1), jnp.where(lane < 64, t1, t2), jnp.where(lane < 32, t2, t3)]
            for m in range(3):
                out[s, :, pl.ds(384 * g + 128 * m, 128)] = jnp.where(alive, dense[m], 0.0)[0:4].astype(BF16)
        return 0

    lax.fori_loop(0, XB, select, 0)


def local(
    features, lengths, stored_slot, owner_slot, gain_first, conv_first, bias_first,
    gain_second, conv_second, bias_second, reduce_conv_weight, reduce_conv_bias,
):
    slots, frames, rows, lanes = features.shape
    feat = jnp.transpose(features, (0, 2, 1, 3)).reshape(slots, rows * frames, lanes)
    hbm = pl.BlockSpec(memory_space=pltpu.HBM)
    dma = pltpu.SemaphoreType.DMA
    result = pl.pallas_call(
        kernel,
        out_shape=jax.ShapeDtypeStruct((slots, frames, 4992), BF16),
        in_specs=[pl.BlockSpec(memory_space=pl.ANY)] + [hbm] * 11,
        out_specs=pl.BlockSpec(memory_space=pltpu.VMEM),
        scratch_shapes=[
            pltpu.VMEM((16, 8, WIN * CH), BF16),
            pltpu.VMEM((WIN, 9, 16, LANES), BF16),
            pltpu.VMEM((3, WIN, 10, 16, LANES), BF16),
            pltpu.VMEM((3, BC, 11, 16, LANES), BF16),
            pltpu.VMEM((9, 512, 256), BF16),
            pltpu.VMEM((9, 512, 256), BF16),
            pltpu.VMEM((1152, 128), BF16),
            pltpu.VMEM((OC, 9, 16, LANES), BF16),
            pltpu.VMEM((XB, 4, 7, 8, LANES), BF16),
            pltpu.VMEM((2 * XB, YB, 7, 8, LANES), BF16),
            pltpu.VMEM((2, WIN, 16, LANES), BF16),
            pltpu.VMEM((3, BC, 16, LANES), BF16),
            pltpu.VMEM((27, CH, CH), BF16),
            pltpu.VMEM((27, CH, CH), BF16),
            pltpu.VMEM((9, CH, CH), BF16),
            pltpu.VMEM((5, 1, CH), F32),
            pltpu.VMEM((8, LANES), F32),
            pltpu.VMEM((256, 256), BF16),
            pltpu.SMEM((8,), jnp.int32),
            pltpu.SMEM((8,), jnp.int32),
            pltpu.SMEM((8,), jnp.int32),
            dma((3, 16)),
            dma((3, 16)),
            dma((34,)),
            dma((34,)),
            dma((4, 8)),
            dma((8, 4)),
            dma((2,)),
            dma((11,)),
        ],
        compiler_params=pltpu.CompilerParams(
            collective_id=0, has_side_effects=True, vmem_limit_bytes=105 << 19
        ),
        name="encode",
    )(
        feat,
        conv_first.reshape(27, CH, CH),
        conv_second.reshape(27, CH, CH),
        reduce_conv_weight.reshape(9, CH, CH),
        *[v.reshape(1, CH) for v in (gain_first, bias_first, gain_second, bias_second, reduce_conv_bias)],
        lengths, stored_slot, owner_slot,
    )
    return result.reshape(slots, frames, 1, 4992)


def solution(mesh):
    spec = P("clip", "tm", "rows", None)
    return jax.shard_map(
        local, mesh=mesh, in_specs=(spec,) + (P(),) * 11, out_specs=spec, check_vma=False
    )
```

```python
import jax
import jax.numpy as jnp
from jax import lax
from jax.experimental import pallas as pl
from jax.experimental.pallas import tpu as pltpu
from jax.sharding import PartitionSpec as P

NORM_EPS = 1e-06
MESH = pl.DeviceIdType.MESH
F32 = jnp.float32
BF16 = jnp.bfloat16

CH = 96
XB = 4
YB = 4
ZB = 8
OWN = 26
GROUPS = 9
WIN = GROUPS * 4
LANES = 128
PAIRS1 = 15
PAIRS2 = 14
BC = 2 * PAIRS1
OC = 2 * PAIRS2
JC = 13


def shifted(flat, step, frame):
    return jnp.where(frame < step, 0.0, pltpu.roll(flat, step, 0))


def split_square(v):
    sq = v * v
    hi = sq.astype(BF16)
    return hi, (sq - hi.astype(F32)).astype(BF16)


def scaled_act(v, total, half_gain):
    half = v * lax.rsqrt(total * (1.0 / CH) + NORM_EPS) * half_gain
    return half + half * jnp.tanh(half)


def build_toeplitz(w_ref, wt):
    def tap(i, _):
        for n in range(2):
            for k in range(3):
                wt[i, pl.ds(128 * (n + k), CH), pl.ds(128 * n, CH)] = w_ref[3 * i + k]
        return 0

    lax.fori_loop(0, 9, tap, 0)


def conv_lhs(src, col0, pairs, rows):
    parts = []
    for t in range(3):
        for j in range(3):
            for k in range(4):
                pieces = []
                for p in range(pairs):
                    for first, count in rows:
                        block = src[t, col0 + 2 * p + k, first + j : first + j + count]
                        pieces.append(block.reshape(count * 16, LANES))
                parts.append(jnp.concatenate(pieces, axis=0))
    return jnp.concatenate(parts, axis=1)


INNER = ((1, 6),)
ORDER = (4, 5, 2, 6, 3, 7, 1, 0)
AROUND = sorted(
    ((dx, dy) for dx in range(4) for dy in range(4) if dx or dy),
    key=lambda d: -(min(d[0], 4 - d[0]) + min(d[1], 4 - d[1])),
)
EDGES = ((0, 1), (7, 1))
EDGES2 = ((0, 1), (7, 2))


def kernel(
    feat, w1h, w2h, wrh, g1h, b1h, g2h, b2h, brh, lenh, stoh, ownh, out,
    arr, xs, a, b, wt1, wt2, rw, ob, sb, gb, ha, hb, w1, w2, wr, vin, vec, ones2,
    lengths, stored, owner,
    s_a, r_a, s_z, r_z, s_g, r_g, l_a, l_w,
):
    x = lax.axis_index("tm")
    zy = lax.axis_index("rows")
    core = lax.axis_index("clip")
    z, y = zy // YB, zy % YB
    me = x * YB + y
    up = ((z + ZB - 1) % ZB) * YB + y
    down = ((z + 1) % ZB) * YB + y

    def plane(i):
        t = (me + i) % 16
        return t, (t // YB, z * YB + t % YB, core)

    def start_lane(q):
        return 2304 * q + 128 * (q // 2 - q // 3)

    def place(q):
        return 384 * (1 - (q + 3) // 4) + 128 * (q // 2 - q // 3)

    arr[:, :, 0:384] = jnp.zeros((16, 8, 384), BF16)
    arr[:, :, 3072:3456] = jnp.zeros((16, 8, 384), BF16)
    barrier = pltpu.get_barrier_semaphore()

    xs_of = [(x + d) % XB for d in range(XB)]
    ys_of = [(y + d) % YB for d in range(YB)]
    for dx in range(XB):
        for dy in range(YB):
            if dx or dy:
                dev = (xs_of[dx], z * YB + ys_of[dy], core)
                pl.semaphore_signal(barrier, inc=1, device_id=dev, device_id_type=MESH)
    for dev in ((x, up, core), (x, down, core), (x, zy, 1 - core)):
        pl.semaphore_signal(barrier, inc=1, device_id=dev, device_id_type=MESH)

    loads = [
        pltpu.make_async_copy(src, dst, l_w.at[i])
        for i, (src, dst) in enumerate(
            [(w1h, w1), (w2h, w2), (wrh, wr)]
            + [(v, vin.at[i]) for i, v in enumerate((g1h, b1h, g2h, b2h, brh))]
            + [(lenh, lengths), (stoh, stored), (ownh, owner)]
        )
    ]
    for c in loads:
        c.start()

    def zero_weights(i, _):
        wt1[i] = jnp.zeros((512, 256), BF16)
        wt2[i] = jnp.zeros((512, 256), BF16)
        return 0

    lax.fori_loop(0, 9, zero_weights, 0)
    rw[...] = jnp.zeros_like(rw)
    vec[...] = jnp.zeros_like(vec)
    r_i = lax.broadcasted_iota(jnp.int32, (256, 256), 0) // 128
    c_i = lax.broadcasted_iota(jnp.int32, (256, 256), 1) // 128
    ones2[...] = jnp.where(r_i == c_i, 1.0, 0.0).astype(BF16)
    loads[0].wait()
    build_toeplitz(w1, wt1)
    pl.semaphore_wait(barrier, 18)

    HALF = 1024

    starts = [start_lane(v) for v in ys_of]
    offs = [place(v) for v in ys_of]

    def in_copy(dx, dy, chunk):
        src = feat.at[xs_of[dx], :, pl.ds(pl.multiple_of(starts[dy] + HALF * chunk, 128), HALF)]
        dst = arr.at[me, :, pl.ds(pl.multiple_of(offs[dy] + HALF * chunk, 128), HALF)]
        return pltpu.make_async_remote_copy(
            src_ref=src, dst_ref=dst,
            send_sem=s_a.at[chunk, 4 * dx + dy],
            recv_sem=r_a.at[chunk, 4 * ((4 - dx) % 4) + (4 - dy) % 4],
            device_id=(xs_of[dx], z * YB + ys_of[dy], core), device_id_type=MESH,
        )

    my_off = place(y)
    own_in = pltpu.make_async_copy(
        feat.at[x, :, pl.ds(pl.multiple_of(start_lane(y), 128), 3 * HALF)],
        arr.at[me, :, pl.ds(pl.multiple_of(my_off, 128), 3 * HALF)],
        l_a.at[0],
    )
    own_in.start()

    def start_in(chunk, _):
        for dx, dy in AROUND:
            in_copy(dx, dy, chunk).start()
        return 0

    lax.fori_loop(0, 3, start_in, 0)

    for c in loads[1:]:
        c.wait()
    build_toeplitz(w2, wt2)

    def tap(i, _):
        rw[pl.ds(pl.multiple_of(128 * i, 128), CH), pl.ds(0, CH)] = wr[i]
        return 0

    lax.fori_loop(0, 9, tap, 0)
    for i in range(5):
        vec[i : i + 1, 0:CH] = vin[i]
    gain1, bias1, gain2, bias2, bias_r = [vec[i : i + 1] for i in range(5)]
    gain1, gain2 = 0.5 * gain1, 0.5 * gain2
    bias1w = jnp.concatenate([bias1, bias1], axis=1)
    gain2w = jnp.concatenate([gain2, gain2], axis=1)
    bias2w = jnp.concatenate([bias2, bias2], axis=1)

    own_in.wait()

    def wait_in(chunk):
        for dx, dy in AROUND:
            t = YB * xs_of[dx] + ys_of[dy]
            dst = arr.at[t, :, pl.ds(pl.multiple_of(my_off + HALF * chunk, 128), HALF)]
            pltpu.make_async_remote_copy(
                src_ref=feat.at[0, :, pl.ds(0, HALF)], dst_ref=dst,
                send_sem=s_a.at[chunk, 4 * dx + dy], recv_sem=r_a.at[chunk, 4 * dx + dy],
                device_id=(xs_of[dx], z * YB + ys_of[dy], core), device_id_type=MESH,
            ).wait_recv()

    lane = lax.broadcasted_iota(jnp.int32, (8, LANES), 1)
    sub8 = lax.broadcasted_iota(jnp.int32, (8, LANES), 0)
    ones1 = jnp.ones((256, LANES), BF16)
    frame128 = lax.broadcasted_iota(jnp.int32, (128, LANES), 0) % 16

    def act_group(q, g):
        lane0 = pl.multiple_of(g * 384, 128)
        cols = [[] for _ in range(4)]
        for xb in range(XB):
            v = [arr[XB * xb + q, :, pl.ds(lane0 + 128 * m, 128)].astype(F32) for m in range(3)]
            cols[0].append(jnp.where(lane < 96, v[0], 0.0))
            cols[1].append(
                jnp.where(lane < 32, pltpu.roll(v[0], 32, 1), jnp.where(lane < 96, pltpu.roll(v[1], 32, 1), 0.0))
            )
            cols[2].append(
                jnp.where(lane < 64, pltpu.roll(v[1], 64, 1), jnp.where(lane < 96, pltpu.roll(v[2], 64, 1), 0.0))
            )
            cols[3].append(jnp.where(lane < 96, pltpu.roll(v[2], 96, 1), 0.0))
        tiles = []
        for c in cols:
            turned = [pltpu.roll(u, 4, 0) for u in c]
            tiles += [jnp.where(sub8 < 4, c[0], turned[1]), jnp.where(sub8 < 4, c[2], turned[3])]
            tiles += [jnp.where(sub8 < 4, turned[0], c[1]), jnp.where(sub8 < 4, turned[2], c[3])]
        return jnp.concatenate(tiles, axis=0)

    def act_store(flat, total, q, g):
        w0 = 4 * g
        row = 2 * q
        xs[pl.ds(w0, 4), pl.ds(row, 2)] = flat.astype(BF16).reshape(4, 2, 16, LANES)
        act = scaled_act(flat, total, gain1)
        for t in range(3):
            moved = act if t == 2 else shifted(act, 2 - t, frame128)
            a[t, pl.ds(w0, 4), pl.ds(row + 1, 2)] = moved.astype(BF16).reshape(4, 2, 16, LANES)

    def act_step(i, qs):
        flats = [act_group(q, i) for q in qs]
        hi, lo = split_square(jnp.concatenate(flats, axis=0))
        total = jnp.dot(jnp.concatenate([hi, lo], axis=1), ones1, preferred_element_type=F32)
        for m, q in enumerate(qs):
            act_store(flats[m], total[128 * m : 128 * m + 128], q, i)
        return 0

    def z_copy(src, dst, k, row):
        return pltpu.make_async_remote_copy(
            src_ref=src, dst_ref=dst, send_sem=s_z.at[k], recv_sem=r_z.at[k],
            device_id=(x, row, core), device_id_type=MESH,
        )

    inside = (z > 0, z < ZB - 1)

    def fill_halo(halo, dst, count, unit, sides):
        frame = lax.broadcasted_iota(jnp.int32, (16 * unit, LANES), 0) % 16

        def step(i, _):
            c = unit * i
            for side, row in enumerate(sides):
                v = halo[side, pl.ds(c, unit)].astype(F32).reshape(16 * unit, LANES)
                v = jnp.where(inside[min(side, 1)], v, 0.0)
                for t in range(3):
                    moved = v if t == 2 else shifted(v, 2 - t, frame)
                    dst[t, pl.ds(c, unit), row] = moved.astype(BF16).reshape(unit, 16, LANES)
            return 0

        lax.fori_loop(0, count // unit, step, 0)

    base = 2 * (1 - y % 2) + 4 * (y // 3)
    col0 = OWN * y

    def conv1(p0, pairs, rows):
        acc = jnp.dot(
            conv_lhs(a, base + 2 * p0, pairs, rows), wt1[...].reshape(4608, 256), preferred_element_type=F32
        )
        v = acc + bias1w
        hi, lo = split_square(v)
        total = jnp.dot(hi, ones2[...], preferred_element_type=F32) + jnp.dot(
            lo, ones2[...], preferred_element_type=F32
        )
        act = scaled_act(v, total, gain2w)
        height = sum(count for _, count in rows)
        m = 16 * height
        frame = lax.broadcasted_iota(jnp.int32, (m, LANES), 0) % 16
        for p in range(pairs):
            for n in range(2):
                bcol = 2 * (p0 + p) + n
                image = col0 - 1 + bcol
                u = act[m * p : m * p + m, 128 * n : 128 * n + 128]
                u = jnp.where(jnp.logical_and(image >= 0, image < 104), u, 0.0)
                for t in range(3):
                    moved = (u if t == 2 else shifted(u, 2 - t, frame)).astype(BF16)
                    at = 0
                    for first, count in rows:
                        b[t, bcol, first + 1 : first + 1 + count] = moved[16 * at : 16 * (at + count)].reshape(
                            count, 16, LANES
                        )
                        at += count

    def conv2(p0, pairs, rows):
        acc = jnp.dot(
            conv_lhs(b, 2 * p0, pairs, rows), wt2[...].reshape(4608, 256), preferred_element_type=F32
        )
        v = acc + bias2w
        height = sum(count for _, count in rows)
        m = 16 * height
        for p in range(pairs):
            for n in range(2):
                c = 2 * (p0 + p) + n
                u = v[m * p : m * p + m, 128 * n : 128 * n + 128]
                at = 0
                for first, count in rows:
                    part = u[16 * at : 16 * (at + count)]
                    part = part + xs[base + 2 + c, first : first + count].reshape(16 * count, LANES).astype(F32)
                    part = jnp.where(col0 + c < 104, part, 0.0).astype(BF16).reshape(count, 16, LANES)
                    if first + count == 9:
                        ob[c, first : first + count - 1] = part[: count - 1]
                        ob[c, 8:9] = jnp.where(z < ZB - 1, part[count - 1 :], 0.0).astype(BF16)
                    else:
                        ob[c, first : first + count] = part
                    at += count

    def inner1(i, _):
        conv1(5 * i, 5, INNER)
        return 0

    def a_copies(g):
        part = pl.ds(4 * g, 4)
        return (
            z_copy(a.at[2, part, 1], ha.at[1, part], g, up),
            z_copy(a.at[2, part, 8], ha.at[0, part], 9 + g, down),
            z_copy(xs.at[part, 0], xs.at[part, 8], 18 + g, up),
        )

    def all_rows(g, _):
        act_step(g, (0, 1, 2, 3))
        for c in a_copies(g):
            c.start()
        return 0

    def chunk_step(chunk, _):
        wait_in(chunk)
        g0, g1 = chunk * (chunk + 3) // 2, (chunk + 1) * (chunk + 4) // 2
        lax.fori_loop(g0, g1, all_rows, 0)
        p0 = jnp.maximum(chunk - 1, 0)
        lax.fori_loop(p0 * (p0 + 1) // 2, chunk * (chunk + 1) // 2, inner1, 0)
        return 0

    lax.fori_loop(0, 3, chunk_step, 0)
    early_b = z_copy(b.at[2, :, 2], hb.at[2], 33, up)
    early_b.start()

    def got_a(g, _):
        for c in a_copies(g)[:2]:
            c.wait_recv()
        return 0

    lax.fori_loop(0, GROUPS, got_a, 0)
    fill_halo(ha, a, WIN, 4, (0, 9))

    def b_copies(e):
        part = pl.ds(10 * e, 10)
        return (
            z_copy(b.at[2, part, 1], hb.at[1, part], 27 + e, up),
            z_copy(b.at[2, part, 8], hb.at[0, part], 30 + e, down),
        )

    def edge1(e, _):
        conv1(5 * e, 5, EDGES)
        for c in b_copies(e):
            c.start()
        return 0

    lax.fori_loop(0, 3, edge1, 0)

    def inner2(i, _):
        conv2(7 * i, 7, INNER)
        return 0

    lax.fori_loop(0, 2, inner2, 0)

    def reduce_rows(rows):
        pieces = []
        for j2 in range(3):
            for k in range(3):
                tiles = []
                for j in range(14):
                    c = min(2 * j + k, OC - 1)
                    tiles += [ob[c, 2 * i + j2] for i in rows]
                pieces.append(jnp.concatenate(tiles, axis=0))
        acc = jnp.dot(jnp.concatenate(pieces, axis=1), rw[...], preferred_element_type=F32) + bias_r
        m = 16 * len(rows)
        for n, i in enumerate(rows):
            for jj in range(7):
                for h in range(2):
                    at = 2 * jj * m + 16 * n + 8 * h
                    e, o = acc[at : at + 8], acc[at + m : at + m + 8]
                    sb[2 * h, i, jj] = jnp.where(sub8 < 4, e, pltpu.roll(o, 4, 0)).astype(BF16)
                    sb[2 * h + 1, i, jj] = jnp.where(sub8 < 4, pltpu.roll(e, 4, 0), o).astype(BF16)

    slot = XB * core + x

    def out_copy(i, k):
        xb = xs_of[ORDER[k] // 2]
        c = core if ORDER[k] % 2 == 0 else 1 - core
        return pltpu.make_async_remote_copy(
            src_ref=sb.at[xb, i], dst_ref=gb.at[slot, y], send_sem=s_g.at[i, k], recv_sem=r_g.at[slot, y],
            device_id=(xb, z * YB + i, c), device_id_type=MESH,
        )

    def each_out(i, act):
        for k in range(8):
            if ORDER[k]:
                act(out_copy(i, k))
            else:

                @pl.when(y != i)
                def _():
                    act(out_copy(i, k))

    def start_out(i):
        each_out(i, lambda c: c.start())

    reduce_rows((1, 2))
    start_out(1)
    start_out(2)
    early_b.wait_recv()

    def got_b(e, _):
        for c in b_copies(e):
            c.wait_recv()
        return 0

    lax.fori_loop(0, 3, got_b, 0)

    def got_x(g, _):
        a_copies(g)[2].wait_recv()
        return 0

    lax.fori_loop(0, GROUPS, got_x, 0)
    fill_halo(hb, b, BC, 5, (0, 9, 10))

    def edge2(i, _):
        conv2(7 * i, 7, EDGES2)
        return 0

    lax.fori_loop(0, 2, edge2, 0)
    reduce_rows((0, 3))
    start_out(0)
    start_out(3)
    own_out = pltpu.make_async_copy(sb.at[x, y], gb.at[slot, y], l_a.at[1])
    own_out.start()
    own_out.wait()

    def wait_out(k, _):
        s, q = k // YB, k % YB

        @pl.when(jnp.logical_not(jnp.logical_and(s == slot, q == y)))
        def _():
            pltpu.make_async_remote_copy(
                src_ref=sb.at[0, 0], dst_ref=gb.at[s, q], send_sem=s_g.at[0, 0], recv_sem=r_g.at[s, q],
                device_id=(x, zy, 1 - core), device_id_type=MESH,
            ).wait_recv()

        return 0

    def end_in(chunk, _):
        for dx, dy in AROUND:
            in_copy(dx, dy, chunk).wait_send()
        return 0

    lax.fori_loop(0, 3, end_in, 0)
    for i in range(4):
        each_out(i, lambda c: c.wait_send())

    def end_rows(g, _):
        for c in a_copies(g):
            c.wait_send()
        return 0

    lax.fori_loop(0, GROUPS, end_rows, 0)

    def end_b(e, _):
        for c in b_copies(e):
            c.wait_send()
        return 0

    lax.fori_loop(0, 3, end_b, 0)
    early_b.wait_send()
    lax.fori_loop(0, 32, wait_out, 0)

    def select(s, _):
        src = jnp.int32(0)
        length = jnp.int32(0)
        for c in range(8):
            hit = owner[c] == XB * core + s
            src = jnp.where(hit, stored[c], src)
            length = jnp.where(hit, lengths[c], length)
        alive = (XB * x + sub8 % 4) < length
        columns = []
        for q in range(YB):
            tiles = gb[src, q]
            for j in range(JC):
                tile = tiles[j // 2].astype(F32)
                columns.append(tile if j % 2 == 0 else pltpu.roll(tile, 4, 0))
        for g in range(13):
            c0, c1, c2, c3 = columns[4 * g : 4 * g + 4]
            t1, t2, t3 = pltpu.roll(c1, 96, 1), pltpu.roll(c2, 64, 1), pltpu.roll(c3, 32, 1)
            dense = [jnp.where(lane < 96, c0, t1), jnp.where(lane < 64, t1, t2), jnp.where(lane < 32, t2, t3)]
            for m in range(3):
                out[s, :, pl.ds(384 * g + 128 * m, 128)] = jnp.where(alive, dense[m], 0.0)[0:4].astype(BF16)
        return 0

    lax.fori_loop(0, XB, select, 0)


def local(
    features, lengths, stored_slot, owner_slot, gain_first, conv_first, bias_first,
    gain_second, conv_second, bias_second, reduce_conv_weight, reduce_conv_bias,
):
    slots, frames, rows, lanes = features.shape
    feat = jnp.transpose(features, (0, 2, 1, 3)).reshape(slots, rows * frames, lanes)
    hbm = pl.BlockSpec(memory_space=pltpu.HBM)
    dma = pltpu.SemaphoreType.DMA
    result = pl.pallas_call(
        kernel,
        out_shape=jax.ShapeDtypeStruct((slots, frames, 4992), BF16),
        in_specs=[pl.BlockSpec(memory_space=pl.ANY)] + [hbm] * 11,
        out_specs=pl.BlockSpec(memory_space=pltpu.VMEM),
        scratch_shapes=[
            pltpu.VMEM((16, 8, WIN * CH), BF16),
            pltpu.VMEM((WIN, 9, 16, LANES), BF16),
            pltpu.VMEM((3, WIN, 10, 16, LANES), BF16),
            pltpu.VMEM((3, BC, 11, 16, LANES), BF16),
            pltpu.VMEM((9, 512, 256), BF16),
            pltpu.VMEM((9, 512, 256), BF16),
            pltpu.VMEM((1152, 128), BF16),
            pltpu.VMEM((OC, 9, 16, LANES), BF16),
            pltpu.VMEM((XB, 4, 7, 8, LANES), BF16),
            pltpu.VMEM((2 * XB, YB, 7, 8, LANES), BF16),
            pltpu.VMEM((2, WIN, 16, LANES), BF16),
            pltpu.VMEM((3, BC, 16, LANES), BF16),
            pltpu.VMEM((27, CH, CH), BF16),
            pltpu.VMEM((27, CH, CH), BF16),
            pltpu.VMEM((9, CH, CH), BF16),
            pltpu.VMEM((5, 1, CH), F32),
            pltpu.VMEM((8, LANES), F32),
            pltpu.VMEM((256, 256), BF16),
            pltpu.SMEM((8,), jnp.int32),
            pltpu.SMEM((8,), jnp.int32),
            pltpu.SMEM((8,), jnp.int32),
            dma((3, 16)),
            dma((3, 16)),
            dma((34,)),
            dma((34,)),
            dma((4, 8)),
            dma((8, 4)),
            dma((2,)),
            dma((11,)),
        ],
        compiler_params=pltpu.CompilerParams(
            collective_id=0, has_side_effects=True, vmem_limit_bytes=105 << 19
        ),
        name="encode",
    )(
        feat,
        conv_first.reshape(27, CH, CH),
        conv_second.reshape(27, CH, CH),
        reduce_conv_weight.reshape(9, CH, CH),
        *[v.reshape(1, CH) for v in (gain_first, bias_first, gain_second, bias_second, reduce_conv_bias)],
        lengths, stored_slot, owner_slot,
    )
    return result.reshape(slots, frames, 1, 4992)


def solution(mesh):
    spec = P("clip", "tm", "rows", None)
    return jax.shard_map(
        local, mesh=mesh, in_specs=(spec,) + (P(),) * 11, out_specs=spec, check_vma=False
    )
```
